32 devices in a mesh: blk: 8 (over z, x), map: 4 (over y, core).
Axes of the slice: x: 2, y: 2, z: 4, core: 2. Of those that a mesh axis runs over, the one named last changes fastest.
Arguments:
- sky_maps: bfloat16 [32, 10, 32768], P(('blk', 'map')), may hold values from -6 to 6
- cycle_number: int32 [32], replicated, may hold values from 8192 to 24576
- legendre_starts: float32 [2, 512, 64, 32], P(None, 'blk', 'map'), may hold values from -6 to 6
Outputs:
- harmonics: bfloat16 [512, 20, 8192], P('blk', None, 'map')
- spectra: float32 [4, 10, 10, 2048], P('map', None, None, 'blk')
The draws below stay inside these ranges and needn't reach their ends.
All inputs are finite; a program needn't handle non-finite values.
Results may differ from the reference program's by a relative error of at most 0.0071.
Values may be sent and summed in bfloat16 or wider, within the bound.
A program may use at most 128 MiB of HBM per device.

```python
import math
import jax
import jax.numpy as jnp
from jax import lax

NSIDE = 8192
CYCLE_LEN = 32768
NMAPS = 10
RES = 128
MGRP = 4
MSTART = 4096
LSTART = 8192
L = 8192
LBLK = 128
CYCLES = 32
N_MAP = 4


def place_ends(values, rng, low, top_value):
    extent = values.shape
    index_at = [jax.random.randint(jax.random.fold_in(rng, axis), (), 0, extent[axis]) for axis in range(len(extent))]
    values = values.at[tuple(index_at)].set(low)
    longest = extent.index(max(extent))
    index_at[longest] = (index_at[longest] + 1) % extent[longest]
    return values.at[tuple(index_at)].set(top_value)


def block_scale(rng, extent, pieces, least, largest):
    loudness, own = 1.0, jax.random.fold_in(rng, 6)
    for position, blocks in pieces:
        steps = jnp.exp(jax.random.uniform(jax.random.fold_in(own, position), (blocks,), jnp.float32, least / len(pieces), largest / len(pieces)))
        loudness = loudness * jnp.repeat(steps, extent[position] // blocks).reshape([-1 if axis == position else 1 for axis in range(len(extent))])
    return loudness


def gaussian(key, shape, scale, limit, cuts=(), kind=jnp.bfloat16):
    level = block_scale(key, shape, cuts, -0.22, 0.18) if cuts else 1.0
    values = jax.random.normal(key, shape, jnp.float32) * scale * level
    return jnp.minimum(jnp.maximum(values, -limit), limit).astype(kind)


def setup_inputs(seed: int = 0) -> dict:
    keys = jax.random.split(jax.random.key(seed), 4)
    sky_maps = gaussian(keys[0], (CYCLES, NMAPS, CYCLE_LEN), 1.0, 6.0, ((0, 32),))
    cycle_number = place_ends(jax.random.randint(keys[1], (CYCLES,), NSIDE, 3 * NSIDE + 1), jax.random.fold_in(keys[1], 1), NSIDE, 3 * NSIDE).astype(jnp.int32)
    legendre_starts = gaussian(keys[2], (2, MGRP * RES, L // LBLK, CYCLES), 1.0, 6.0, ((1, 8), (2, 4)), jnp.float32)
    return {"sky_maps": sky_maps, "cycle_number": cycle_number, "legendre_starts": legendre_starts}


def cycle_height(cycle_ids):
    return (4.0 * NSIDE - 2.0 * cycle_ids.astype(jnp.float32)) / (3.0 * NSIDE)

def dft_tables(cycle_len):
    low_len = cycle_len // RES
    residue = jnp.arange(RES, dtype=jnp.int32)
    turn_one = residue[:, None] * residue[None, :] % RES
    angle_one = 2.0 * math.pi / RES * turn_one.astype(jnp.float32)
    first_table = jnp.concatenate([jnp.cos(angle_one), -jnp.sin(angle_one)], axis=1).astype(jnp.bfloat16)
    column_group = jnp.arange(MGRP, dtype=jnp.int32)
    sample = jnp.arange(low_len, dtype=jnp.int32)
    m_value = MSTART + RES * column_group[:, None, None] + residue[None, None, :]
    turn_two = m_value * sample[None, :, None] % cycle_len
    angle_two = 2.0 * math.pi / cycle_len * turn_two.astype(jnp.float32)
    twiddle_re = jnp.cos(angle_two).astype(jnp.bfloat16)
    twiddle_im = (-jnp.sin(angle_two)).astype(jnp.bfloat16)
    return (first_table, twiddle_re, twiddle_im)

def cycle_transform(cycle_rows, parity, tables):
    first_table, twiddle_re, twiddle_im = tables
    cycle_count, maps_count, cycle_len = cycle_rows.shape
    low_len = cycle_len // RES
    folded = cycle_rows.reshape(cycle_count, maps_count, RES, low_len).astype(jnp.float32)
    section_one = jnp.einsum('rnaj,ak->rnjk', folded, first_table.astype(jnp.float32))
    section_one = lax.optimization_barrier(section_one.astype(jnp.bfloat16)).astype(jnp.float32)
    part_re = section_one[..., :RES]
    part_im = section_one[..., RES:]
    wave_re = twiddle_re.astype(jnp.float32)
    wave_im = twiddle_im.astype(jnp.float32)
    real_sum = jnp.einsum('rnjk,cjk->rnck', part_re, wave_re) - jnp.einsum('rnjk,cjk->rnck', part_im, wave_im)
    imag_sum = jnp.einsum('rnjk,cjk->rnck', part_im, wave_re) + jnp.einsum('rnjk,cjk->rnck', part_re, wave_im)
    column_group = jnp.arange(MGRP, dtype=jnp.int32)
    residue = jnp.arange(RES, dtype=jnp.int32)
    m_value = MSTART + RES * column_group[:, None] + residue[None, :]
    shifted = m_value[None, :, :] * parity[:, None, None] % (2 * cycle_len)
    phase_angle = math.pi / cycle_len * shifted.astype(jnp.float32)
    cos_part = jnp.cos(phase_angle)[:, None]
    sin_part = jnp.sin(phase_angle)[:, None]
    factor = 1.0 / math.sqrt(cycle_len)
    out_re = factor * (cos_part * real_sum + sin_part * imag_sum)
    out_im = factor * (cos_part * imag_sum - sin_part * real_sum)
    return jnp.stack([out_re, out_im], axis=1).astype(jnp.bfloat16)

def legendre_rows(start_pair, height, m_float, first_l):
    m_column = m_float[:, None]

    def recur_coef(degree):
        return jnp.sqrt((4.0 * degree * degree - 1.0) / ((degree - m_column) * (degree + m_column)))
    base_l = first_l.astype(jnp.float32)
    value_older = start_pair[0]
    value_newer = start_pair[1]
    prior_coef = recur_coef(base_l - 1.0)
    height_row = height[None, :]
    stacked_rows = []
    for offset in range(LBLK):
        present_coef = recur_coef(base_l + offset)
        value_now = present_coef * (height_row * value_newer - value_older / prior_coef)
        stacked_rows.append(value_now)
        value_older = value_newer
        value_newer = value_now
        prior_coef = present_coef
    return jnp.stack(stacked_rows, axis=1)

def reference(sky_maps, cycle_number, legendre_starts):
    cycle_count, maps_count, cycle_len = sky_maps.shape
    tables = dft_tables(cycle_len)
    parity = (cycle_number - NSIDE + 1) % 2
    block_rows = 8
    folded_maps = sky_maps.reshape(cycle_count // block_rows, block_rows, maps_count, cycle_len)
    folded_parity = parity.reshape(cycle_count // block_rows, block_rows)

    def transform_block(inputs):
        return cycle_transform(inputs[0], inputs[1], tables)
    cycle_modes = lax.map(transform_block, (folded_maps, folded_parity))
    cycle_modes = cycle_modes.reshape(cycle_count, 2, maps_count, MGRP, RES)
    total_cols = MGRP * RES
    ordered = jnp.transpose(cycle_modes, (4, 3, 1, 2, 0)).reshape(total_cols, 2 * maps_count, cycle_count)
    modes_wide = ordered.astype(jnp.float32)
    heights = cycle_height(cycle_number)
    column = jnp.arange(total_cols, dtype=jnp.int32)
    m_float = (MSTART + RES * (column % MGRP) + column // MGRP).astype(jnp.float32)
    cycle_scale = 1.0 / math.sqrt(cycle_count)

    def one_block(block_index):
        start_pair = lax.dynamic_index_in_dim(legendre_starts, block_index, 2, keepdims=False)
        first_l = LSTART + block_index * LBLK
        legendre_tile = legendre_rows(start_pair, heights, m_float, first_l)
        legendre_tile = lax.optimization_barrier(legendre_tile.astype(jnp.bfloat16)).astype(jnp.float32)
        projected = jnp.einsum('qlr,qnr->qnl', legendre_tile, modes_wide) * cycle_scale
        return projected.astype(jnp.bfloat16)
    blocks_out = lax.map(one_block, jnp.arange(L // LBLK, dtype=jnp.int32))
    harmonics = jnp.transpose(blocks_out, (1, 2, 0, 3)).reshape(total_cols, 2 * maps_count, L)
    split_harm = harmonics.astype(jnp.float32).reshape(total_cols, 2, maps_count, L)
    cross_sum = jnp.einsum('qcil,qcjl->ijl', split_harm, split_harm) / total_cols
    spectra = jnp.transpose(cross_sum.reshape(maps_count, maps_count, N_MAP, L // N_MAP), (2, 0, 1, 3))
    return (harmonics, spectra)
```

```python
import functools
import math

import jax
import jax.numpy as jnp
from jax import lax
from jax.experimental import pallas as pl
from jax.experimental.pallas import tpu as pltpu
from jax.sharding import PartitionSpec as P

NSIDE = 8192
RES = 128
MGRP = 4
MSTART = 4096
LSTART = 8192
LBLK = 128


def shortened(array):

    def short(part):
        return part.astype(jnp.bfloat16) if part.dtype == jnp.float32 else part

    return jax.tree.map(short, array)


def cycle_height(cycle_ids):
    return (4.0 * NSIDE - 2.0 * cycle_ids.astype(jnp.float32)) / (3.0 * NSIDE)


def dft_tables(cycle_len):
    low_len = cycle_len // RES
    residue = jnp.arange(RES, dtype=jnp.int32)
    turn_one = residue[:, None] * residue[None, :] % RES
    angle_one = 2.0 * math.pi / RES * turn_one.astype(jnp.float32)
    first_table = jnp.concatenate([jnp.cos(angle_one), -jnp.sin(angle_one)], axis=1).astype(
        jnp.bfloat16
    )
    column_group = jnp.arange(MGRP, dtype=jnp.int32)
    sample = jnp.arange(low_len, dtype=jnp.int32)
    m_value = MSTART + RES * column_group[:, None, None] + residue[None, None, :]
    turn_two = m_value * sample[None, :, None] % cycle_len
    angle_two = 2.0 * math.pi / cycle_len * turn_two.astype(jnp.float32)
    twiddle_re = jnp.cos(angle_two).astype(jnp.bfloat16)
    twiddle_im = (-jnp.sin(angle_two)).astype(jnp.bfloat16)
    return (first_table, twiddle_re, twiddle_im)


def cycle_transform(cycle_rows, parity, tables):
    first_table, twiddle_re, twiddle_im = tables
    cycle_count, maps_count, cycle_len = cycle_rows.shape
    low_len = cycle_len // RES
    folded = cycle_rows.reshape(cycle_count, maps_count, RES, low_len)
    section_one = jnp.einsum(
        "rnaj,ak->rnjk", folded, first_table, preferred_element_type=jnp.float32
    )
    section_one = section_one.astype(jnp.bfloat16)
    part_re = section_one[..., :RES]
    part_im = section_one[..., RES:]
    real_sum = jnp.einsum(
        "rnjk,cjk->rnck", part_re, twiddle_re, preferred_element_type=jnp.float32
    ) - jnp.einsum("rnjk,cjk->rnck", part_im, twiddle_im, preferred_element_type=jnp.float32)
    imag_sum = jnp.einsum(
        "rnjk,cjk->rnck", part_im, twiddle_re, preferred_element_type=jnp.float32
    ) + jnp.einsum("rnjk,cjk->rnck", part_re, twiddle_im, preferred_element_type=jnp.float32)
    column_group = jnp.arange(MGRP, dtype=jnp.int32)
    residue = jnp.arange(RES, dtype=jnp.int32)
    m_value = MSTART + RES * column_group[:, None] + residue[None, :]
    shifted = m_value[None, :, :] * parity[:, None, None] % (2 * cycle_len)
    phase_angle = math.pi / cycle_len * shifted.astype(jnp.float32)
    cos_part = jnp.cos(phase_angle)[:, None]
    sin_part = jnp.sin(phase_angle)[:, None]
    factor = 1.0 / math.sqrt(cycle_len)
    out_re = factor * (cos_part * real_sum + sin_part * imag_sum)
    out_im = factor * (cos_part * imag_sum - sin_part * real_sum)
    return jnp.stack([out_re, out_im], axis=1).astype(jnp.bfloat16)


def legendre_rows(start_pair, height, m_float, first_l):
    m_column = m_float[:, None]

    def recur_coef(degree):
        return jnp.sqrt((4.0 * degree * degree - 1.0) / ((degree - m_column) * (degree + m_column)))

    base_l = first_l.astype(jnp.float32)
    value_older = start_pair[0]
    value_newer = start_pair[1]
    prior_coef = recur_coef(base_l - 1.0)
    height_row = height[None, :]
    stacked_rows = []
    for offset in range(LBLK):
        present_coef = recur_coef(base_l + offset)
        value_now = present_coef * (height_row * value_newer - value_older / prior_coef)
        stacked_rows.append(value_now)
        value_older = value_newer
        value_newer = value_now
        prior_coef = present_coef
    return jnp.stack(stacked_rows, axis=1)


STEP_LANES = 512
KDIM = 256
GAP = 8


def spectra_kernel(
    dims, starts_ref, z_ref, m_ref, base_ref, modes_ref, harm_ref, cross_ref,
    p_ref, turned_ref, pieces_ref, kap_ref, leg_ref, acc_ref,
):
    blocks, cycles, maps, q_group, pad_maps, scale = dims
    step = pl.program_id(0)
    groups = STEP_LANES // KDIM
    halves = STEP_LANES // 128
    parts = 2 * maps
    rows_out = q_group * pad_maps

    @pl.when(step == 0)
    def _():
        m_row = m_ref[...]
        piece = lax.broadcasted_iota(jnp.int32, (blocks, 256), 1) // 64

        def setup(j, carry):
            p_prev, q_prev = carry
            degree = base_ref[...] + j.astype(jnp.float32)
            num = 4.0 * degree * degree - 1.0
            den = (degree - m_row) * (degree + m_row)
            root = lax.rsqrt(num * den)
            kappa = p_prev * p_prev
            high = kappa.astype(jnp.bfloat16).astype(jnp.float32)
            rest = kappa - high
            mid = rest.astype(jnp.bfloat16).astype(jnp.float32)
            low = rest - mid
            pieces = jnp.where(piece == 0, high, jnp.where(piece == 1, mid, low))
            pieces_ref[pl.ds(pl.multiple_of(j * blocks, blocks), blocks), :] = pieces.astype(
                jnp.bfloat16
            )
            p_now = num * root * q_prev
            q_now = den * root * p_prev
            for half in range(blocks // 8):
                p_ref[pl.ds(half * 8 * (LBLK + GAP) + j, 8, stride=LBLK + GAP), :] = p_now[
                    half * 8 : half * 8 + 8, :128
                ]
            return p_now, q_now

        one = jnp.ones((blocks, 256), jnp.float32)
        lax.fori_loop(0, LBLK, setup, (one, one), unroll=4)
        acc_ref[...] = jnp.zeros_like(acc_ref)

        def turn(t, _):
            turned_ref[t] = p_ref[pl.ds(pl.multiple_of(t * (LBLK + GAP), 8), LBLK), :].T
            return 0

        lax.fori_loop(0, blocks, turn, 0)

    q_row = lax.broadcasted_iota(jnp.int32, (256, STEP_LANES), 0)
    q_lane = lax.broadcasted_iota(jnp.int32, (256, STEP_LANES), 1) // cycles + step * (
        STEP_LANES // cycles
    )
    spread = jnp.where((q_row % 64 == q_lane) & (q_row < 192), 1.0, 0.0).astype(jnp.bfloat16)

    def widen(i, _):
        rows = pl.ds(pl.multiple_of(i * 256, 256), 256)
        kap_ref[rows, :] = jnp.dot(
            pieces_ref[rows, :], spread, preferred_element_type=jnp.float32
        ) * z_ref[...]
        return 0

    lax.fori_loop(0, blocks * LBLK // 256, widen, 0, unroll=2)

    def recur(j, carry):
        older, newer = carry
        kap = kap_ref[pl.ds(pl.multiple_of(j * blocks, blocks), blocks), :]
        now = kap * newer - older
        for half in range(blocks // 8):
            for g in range(halves):
                leg_ref[g, pl.ds(half * 8 * (LBLK + GAP) + j, 8, stride=LBLK + GAP), :] = now[
                    half * 8 : half * 8 + 8, g * 128 : g * 128 + 128
                ]
        return newer, now

    lax.fori_loop(0, LBLK, recur, (starts_ref[0], starts_ref[1]), unroll=8)

    rows_all = modes_ref.shape[1]
    row = lax.broadcasted_iota(jnp.int32, (rows_all, KDIM), 0)
    lane = lax.broadcasted_iota(jnp.int32, (rows_all, KDIM), 1)
    row_q = jnp.where(row < rows_out, row // pad_maps, (row - rows_out) % q_group)
    same_q = row_q == lane // cycles
    cyc = lax.broadcasted_iota(jnp.int32, (cycles, KDIM), 0)
    lane_c = lax.broadcasted_iota(jnp.int32, (cycles, KDIM), 1) % cycles
    tile = jnp.where(cyc == lane_c, 1.0, 0.0).astype(jnp.bfloat16)
    weights = []
    for g in range(groups):
        wide = jnp.dot(modes_ref[g], tile, preferred_element_type=jnp.float32)
        weights.append(jnp.where(same_q, wide, 0.0).astype(jnp.bfloat16))

    def project(t, _):
        cols = pl.ds(pl.multiple_of(t * LBLK, LBLK), LBLK)
        src = pl.ds(pl.multiple_of(t * (LBLK + GAP), 8), LBLK)
        spectra_rows = []
        for g in range(groups):
            first = pl.multiple_of((step * groups + g) * q_group, 8)
            p_rows = turned_ref[t, pl.ds(first, q_group), :] * scale
            leg = jnp.concatenate(
                [leg_ref[g * (KDIM // 128) + h, src, :] for h in range(KDIM // 128)], axis=1
            ).astype(jnp.bfloat16)
            out = lax.dot_general(
                weights[g], leg, (((1,), (1,)), ((), ())), preferred_element_type=jnp.float32
            )
            direct = out[:rows_out].reshape(q_group, pad_maps, LBLK) * p_rows[:, None, :]
            harm_ref[g * q_group : (g + 1) * q_group, :, cols] = direct[:, :parts].astype(
                jnp.bfloat16
            )
            crossed = out[rows_out:].reshape(parts, q_group, LBLK) * p_rows[None]
            spectra_rows.append(crossed.astype(jnp.bfloat16).astype(jnp.float32))
        pair = 0
        for i in range(maps):
            for k in range(i, maps):
                total = acc_ref[pair, :, cols]
                for x in spectra_rows:
                    total = total + x[i] * x[k] + x[maps + i] * x[maps + k]
                acc_ref[pair, :, cols] = total
                pair += 1
        return 0

    lax.fori_loop(0, blocks, project, 0)

    @pl.when(step == pl.num_programs(0) - 1)
    def _():
        def finish(t, _):
            cols = pl.ds(pl.multiple_of(t * LBLK, LBLK), LBLK)
            cross_ref[:, cols] = jnp.sum(acc_ref[:, :, cols], axis=1)
            return 0

        lax.fori_loop(0, blocks, finish, 0)


def project_blocks(legendre_starts, heights, m_float, first_l, modes, maps_count, cycle_scale):
    local_cols, block_count, cycles = legendre_starts.shape[1:]
    local_len = block_count * LBLK
    q_group = KDIM // cycles
    parts = 2 * maps_count
    pad_maps = -(-parts // 8) * 8
    pairs = maps_count * (maps_count + 1) // 2
    base_l = first_l.astype(jnp.float32) + LBLK * jnp.arange(block_count, dtype=jnp.float32)
    degree = base_l[None, :] - 1.0
    m_col = m_float[:, None]
    coef = jnp.sqrt((4.0 * degree * degree - 1.0) / ((degree - m_col) * (degree + m_col)))
    starts = jnp.stack([legendre_starts[0] / coef[:, :, None], legendre_starts[1]])
    starts = jnp.transpose(starts, (0, 2, 1, 3)).reshape(2, block_count, local_cols * cycles)
    z_row = jnp.tile(heights, STEP_LANES // cycles)[None]
    m_row = jnp.tile(m_float, 256 // local_cols)[None]
    base = jnp.broadcast_to(base_l[:, None], (block_count, 256))
    grouped = modes.reshape(local_cols // q_group, q_group, parts, cycles)
    padded = jnp.pad(grouped, ((0, 0), (0, 0), (0, pad_maps - parts), (0, 0)))
    ordered = jnp.concatenate(
        [
            padded.reshape(local_cols // q_group, q_group * pad_maps, cycles),
            jnp.transpose(grouped, (0, 2, 1, 3)).reshape(
                local_cols // q_group, parts * q_group, cycles
            ),
        ],
        axis=1,
    )
    groups = STEP_LANES // KDIM
    step_cols = groups * q_group
    dims = (block_count, cycles, maps_count, q_group, pad_maps, cycle_scale)
    whole = lambda shape: pl.BlockSpec(shape, lambda i: (0,) * len(shape))
    return pl.pallas_call(
        functools.partial(spectra_kernel, dims),
        grid=(local_cols // step_cols,),
        out_shape=(
            jax.ShapeDtypeStruct((local_cols, parts, local_len), jnp.bfloat16),
            jax.ShapeDtypeStruct((pairs, local_len), jnp.float32),
        ),
        in_specs=[
            pl.BlockSpec((2, block_count, STEP_LANES), lambda i: (0, 0, i)),
            whole((1, STEP_LANES)),
            whole((1, 256)),
            whole((block_count, 256)),
            pl.BlockSpec((groups, ordered.shape[1], cycles), lambda i: (i, 0, 0)),
        ],
        out_specs=(
            pl.BlockSpec((step_cols, parts, local_len), lambda i: (i, 0, 0)),
            whole((pairs, local_len)),
        ),
        scratch_shapes=[
            pltpu.VMEM((block_count * (LBLK + GAP), 128), jnp.float32),
            pltpu.VMEM((block_count, 128, LBLK), jnp.float32),
            pltpu.VMEM((local_len, 256), jnp.bfloat16),
            pltpu.VMEM((local_len, STEP_LANES), jnp.float32),
            pltpu.VMEM((STEP_LANES // 128, block_count * (LBLK + GAP), 128), jnp.float32),
            pltpu.VMEM((pairs, 8, local_len), jnp.float32),
        ],
        compiler_params=pltpu.CompilerParams(vmem_limit_bytes=60 * 1024 * 1024),
    )(starts, z_row, m_row, base, ordered)


def kernel_fits(local_cols, cycles, block_count):
    return cycles == 32 and local_cols == 64 and block_count % 8 == 0


def body(sky_maps, cycle_number, legendre_starts):
    own_cycles, maps_count, cycle_len = sky_maps.shape
    tables = dft_tables(cycle_len)
    map_total = lax.axis_size("map")
    blk_total = lax.axis_size("blk")
    first_row = (lax.axis_index("blk") * map_total + lax.axis_index("map")) * own_cycles
    own_numbers = lax.dynamic_slice_in_dim(cycle_number, first_row, own_cycles)
    parity = (own_numbers - NSIDE + 1) % 2
    local_modes = cycle_transform(sky_maps, parity, tables)
    grouped = lax.all_gather(local_modes, "map", axis=0, tiled=True)
    regrouped = lax.all_to_all(grouped, "blk", split_axis=4, concat_axis=0, tiled=True)
    ordered = jnp.transpose(regrouped, (4, 3, 1, 2, 0))
    local_cols = ordered.shape[0] * ordered.shape[1]
    cycle_modes = ordered.reshape(local_cols, 2 * maps_count, -1)
    heights = cycle_height(cycle_number)
    column = lax.axis_index("blk") * local_cols + jnp.arange(local_cols, dtype=jnp.int32)
    m_float = (MSTART + RES * (column % MGRP) + column // MGRP).astype(jnp.float32)
    block_count = legendre_starts.shape[2]
    local_len = block_count * LBLK
    first_l = LSTART + lax.axis_index("map") * local_len
    cycle_scale = 1.0 / math.sqrt(cycle_modes.shape[-1])

    if kernel_fits(local_cols, cycle_modes.shape[-1], block_count):
        harmonics, cross = project_blocks(
            legendre_starts, heights, m_float, first_l, cycle_modes, maps_count, cycle_scale
        )
        owned = lax.psum_scatter(cross, "blk", scatter_dimension=1, tiled=True)
        pair_of = [[0] * maps_count for _ in range(maps_count)]
        pair = 0
        for i in range(maps_count):
            for k in range(i, maps_count):
                pair_of[i][k] = pair_of[k][i] = pair
                pair += 1
        rows = [owned[pair_of[i][k]] for i in range(maps_count) for k in range(maps_count)]
        spectra = jnp.stack(rows).reshape(maps_count, maps_count, -1) / (MGRP * RES)
        return (harmonics, spectra[None])

    def one_block(block_index):
        start_pair = lax.dynamic_index_in_dim(legendre_starts, block_index, 2, keepdims=False)
        legendre_tile = legendre_rows(
            start_pair, heights, m_float, first_l + block_index * LBLK
        ).astype(jnp.bfloat16)
        projected = (
            jnp.einsum(
                "qlr,qnr->qnl", legendre_tile, cycle_modes, preferred_element_type=jnp.float32
            )
            * cycle_scale
        )
        return projected.astype(jnp.bfloat16)

    blocks_out = lax.map(one_block, jnp.arange(block_count, dtype=jnp.int32))
    harmonics = jnp.transpose(blocks_out, (1, 2, 0, 3)).reshape(
        local_cols, 2 * maps_count, local_len
    )
    total_cols = MGRP * RES
    spread = harmonics.reshape(local_cols, 2 * maps_count, blk_total, local_len // blk_total)
    spread = jnp.transpose(spread, (2, 3, 1, 0))
    received = lax.all_to_all(
        shortened(spread), "blk", split_axis=0, concat_axis=3, tiled=True
    ).astype(spread.dtype)
    item_count = received.shape[1]
    split_piece = received.reshape(item_count, 2, maps_count, received.shape[3])
    cross_sum = jnp.einsum(
        "gciq,gcjq->ijg", split_piece, split_piece, preferred_element_type=jnp.float32
    )
    owned = (cross_sum / total_cols)[None]
    return (harmonics, owned)


def solution(mesh):
    return jax.shard_map(
        body,
        mesh=mesh,
        in_specs=(P(("blk", "map"), None, None), P(), P(None, "blk", "map", None)),
        out_specs=(P("blk", None, "map"), P("map", None, None, "blk")),
        check_vma=False,
    )
```

```python
import functools
import math

import jax
import jax.numpy as jnp
import numpy as np
from jax import lax
from jax.experimental import pallas as pl
from jax.experimental.pallas import tpu as pltpu
from jax.sharding import PartitionSpec as P

NSIDE = 8192
RES = 128
MGRP = 4
MSTART = 4096
LSTART = 8192
LBLK = 128


def shortened(array):

    def short(part):
        return part.astype(jnp.bfloat16) if part.dtype == jnp.float32 else part

    return jax.tree.map(short, array)


def cycle_height(cycle_ids):
    return (4.0 * NSIDE - 2.0 * cycle_ids.astype(jnp.float32)) / (3.0 * NSIDE)


def dft_tables(cycle_len):
    low_len = cycle_len // RES
    residue = jnp.arange(RES, dtype=jnp.int32)
    turn_one = residue[:, None] * residue[None, :] % RES
    angle_one = 2.0 * math.pi / RES * turn_one.astype(jnp.float32)
    first_table = jnp.concatenate([jnp.cos(angle_one), -jnp.sin(angle_one)], axis=1).astype(
        jnp.bfloat16
    )
    column_group = jnp.arange(MGRP, dtype=jnp.int32)
    sample = jnp.arange(low_len, dtype=jnp.int32)
    m_value = MSTART + RES * column_group[:, None, None] + residue[None, None, :]
    turn_two = m_value * sample[None, :, None] % cycle_len
    angle_two = 2.0 * math.pi / cycle_len * turn_two.astype(jnp.float32)
    twiddle_re = jnp.cos(angle_two).astype(jnp.bfloat16)
    twiddle_im = (-jnp.sin(angle_two)).astype(jnp.bfloat16)
    return (first_table, twiddle_re, twiddle_im)


def cycle_transform(cycle_rows, parity, tables):
    first_table, twiddle_re, twiddle_im = tables
    cycle_count, maps_count, cycle_len = cycle_rows.shape
    low_len = cycle_len // RES
    folded = cycle_rows.reshape(cycle_count, maps_count, RES, low_len)
    section_one = jnp.einsum(
        "rnaj,ak->rnjk", folded, first_table, preferred_element_type=jnp.float32
    )
    section_one = section_one.astype(jnp.bfloat16)
    part_re = section_one[..., :RES]
    part_im = section_one[..., RES:]
    real_sum = jnp.einsum(
        "rnjk,cjk->rnck", part_re, twiddle_re, preferred_element_type=jnp.float32
    ) - jnp.einsum("rnjk,cjk->rnck", part_im, twiddle_im, preferred_element_type=jnp.float32)
    imag_sum = jnp.einsum(
        "rnjk,cjk->rnck", part_im, twiddle_re, preferred_element_type=jnp.float32
    ) + jnp.einsum("rnjk,cjk->rnck", part_re, twiddle_im, preferred_element_type=jnp.float32)
    column_group = jnp.arange(MGRP, dtype=jnp.int32)
    residue = jnp.arange(RES, dtype=jnp.int32)
    m_value = MSTART + RES * column_group[:, None] + residue[None, :]
    shifted = m_value[None, :, :] * parity[:, None, None] % (2 * cycle_len)
    phase_angle = math.pi / cycle_len * shifted.astype(jnp.float32)
    cos_part = jnp.cos(phase_angle)[:, None]
    sin_part = jnp.sin(phase_angle)[:, None]
    factor = 1.0 / math.sqrt(cycle_len)
    out_re = factor * (cos_part * real_sum + sin_part * imag_sum)
    out_im = factor * (cos_part * imag_sum - sin_part * real_sum)
    return jnp.stack([out_re, out_im], axis=1).astype(jnp.bfloat16)


def legendre_rows(start_pair, height, m_float, first_l):
    m_column = m_float[:, None]

    def recur_coef(degree):
        return jnp.sqrt((4.0 * degree * degree - 1.0) / ((degree - m_column) * (degree + m_column)))

    base_l = first_l.astype(jnp.float32)
    value_older = start_pair[0]
    value_newer = start_pair[1]
    prior_coef = recur_coef(base_l - 1.0)
    height_row = height[None, :]
    stacked_rows = []
    for offset in range(LBLK):
        present_coef = recur_coef(base_l + offset)
        value_now = present_coef * (height_row * value_newer - value_older / prior_coef)
        stacked_rows.append(value_now)
        value_older = value_newer
        value_newer = value_now
        prior_coef = present_coef
    return jnp.stack(stacked_rows, axis=1)


STEP_LANES = 512
KDIM = 256
GAP = 8


def spectra_kernel(
    dims, starts_ref, z_ref, m_ref, base_ref, modes_ref, harm_ref, cross_ref,
    p_ref, turned_ref, pieces_ref, kap_ref, leg_ref, acc_ref,
):
    blocks, cycles, maps, q_group, scale = dims
    step = pl.program_id(0)
    groups = STEP_LANES // KDIM
    halves = STEP_LANES // 128
    parts = 2 * maps

    @pl.when(step == 0)
    def _():
        m_row = m_ref[...]
        piece = lax.broadcasted_iota(jnp.int32, (blocks, 256), 1) // 64

        def setup(j, carry):
            p_prev, q_prev = carry
            degree = base_ref[...] + j.astype(jnp.float32)
            num = 4.0 * degree * degree - 1.0
            den = (degree - m_row) * (degree + m_row)
            root = lax.rsqrt(num * den)
            kappa = p_prev * p_prev
            high = kappa.astype(jnp.bfloat16).astype(jnp.float32)
            rest = kappa - high
            mid = rest.astype(jnp.bfloat16).astype(jnp.float32)
            low = rest - mid
            pieces = jnp.where(piece == 0, high, jnp.where(piece == 1, mid, low))
            pieces_ref[pl.ds(pl.multiple_of(j * blocks, blocks), blocks), :] = pieces.astype(
                jnp.bfloat16
            )
            p_now = num * root * q_prev
            q_now = den * root * p_prev
            for half in range(blocks // 8):
                p_ref[pl.ds(half * 8 * (LBLK + GAP) + j, 8, stride=LBLK + GAP), :] = p_now[
                    half * 8 : half * 8 + 8, :128
                ]
            return p_now, q_now

        one = jnp.ones((blocks, 256), jnp.float32)
        lax.fori_loop(0, LBLK, setup, (one, one), unroll=4)
        acc_ref[...] = jnp.zeros_like(acc_ref)

        def turn(t, _):
            turned_ref[t] = p_ref[pl.ds(pl.multiple_of(t * (LBLK + GAP), 8), LBLK), :].T
            return 0

        lax.fori_loop(0, blocks, turn, 0)

    q_row = lax.broadcasted_iota(jnp.int32, (256, STEP_LANES), 0)
    q_lane = lax.broadcasted_iota(jnp.int32, (256, STEP_LANES), 1) // cycles + step * (
        STEP_LANES // cycles
    )
    spread = jnp.where((q_row % 64 == q_lane) & (q_row < 192), 1.0, 0.0).astype(jnp.bfloat16)

    def widen(i, _):
        rows = pl.ds(pl.multiple_of(i * 256, 256), 256)
        kap_ref[rows, :] = jnp.dot(
            pieces_ref[rows, :], spread, preferred_element_type=jnp.float32
        ) * z_ref[...]
        return 0

    lax.fori_loop(0, blocks * LBLK // 256, widen, 0, unroll=2)

    def recur(j, carry):
        older, newer = carry
        kap = kap_ref[pl.ds(pl.multiple_of(j * blocks, blocks), blocks), :]
        now = kap * newer - older
        for half in range(blocks // 8):
            for g in range(halves):
                leg_ref[g, pl.ds(half * 8 * (LBLK + GAP) + j, 8, stride=LBLK + GAP), :] = now[
                    half * 8 : half * 8 + 8, g * 128 : g * 128 + 128
                ]
        return newer, now

    lax.fori_loop(0, LBLK, recur, (starts_ref[0], starts_ref[1]), unroll=8)

    rows_all = parts * q_group
    row = lax.broadcasted_iota(jnp.int32, (rows_all, 128), 0)
    lane = lax.broadcasted_iota(jnp.int32, (rows_all, 128), 1)
    picked = (row % MGRP) * parts + row // q_group == lane
    row = lax.broadcasted_iota(jnp.int32, (rows_all, KDIM), 0)
    lane = lax.broadcasted_iota(jnp.int32, (rows_all, KDIM), 1)
    same_q = row % q_group == lane // cycles
    cyc = lax.broadcasted_iota(jnp.int32, (cycles, KDIM), 0)
    lane_c = lax.broadcasted_iota(jnp.int32, (cycles, KDIM), 1) % cycles
    tile = jnp.where(cyc == lane_c, 1.0, 0.0).astype(jnp.bfloat16)
    row_k = lax.broadcasted_iota(jnp.int32, (rows_all, 128), 0) % q_group // MGRP
    per_group = q_group // MGRP
    weights = []
    for g in range(groups):
        narrow = jnp.zeros((rows_all, cycles), jnp.float32)
        for k in range(per_group):
            pick = jnp.where(picked & (row_k == k), 1.0, 0.0).astype(jnp.bfloat16)
            narrow = narrow + lax.dot_general(
                pick, modes_ref[g * per_group + k], (((1,), (1,)), ((), ())),
                preferred_element_type=jnp.float32,
            )
        wide = jnp.dot(narrow.astype(jnp.bfloat16), tile, preferred_element_type=jnp.float32)
        weights.append(jnp.where(same_q, wide, 0.0).astype(jnp.bfloat16))

    def project(t, _):
        cols = pl.ds(pl.multiple_of(t * LBLK, LBLK), LBLK)
        src = pl.ds(pl.multiple_of(t * (LBLK + GAP), 8), LBLK)
        spectra_rows = []
        for g in range(groups):
            first = pl.multiple_of((step * groups + g) * q_group, 8)
            p_rows = turned_ref[t, pl.ds(first, q_group), :] * scale
            leg = jnp.concatenate(
                [leg_ref[g * (KDIM // 128) + h, src, :] for h in range(KDIM // 128)], axis=1
            ).astype(jnp.bfloat16)
            out = lax.dot_general(
                weights[g], leg, (((1,), (1,)), ((), ())), preferred_element_type=jnp.float32
            )
            crossed = out.reshape(parts, q_group, LBLK) * p_rows[None]
            crossed = crossed.astype(jnp.bfloat16)
            harm_ref[:, g * q_group : (g + 1) * q_group, cols] = crossed
            spectra_rows.append(crossed.astype(jnp.float32))
        pair = 0
        for i in range(maps):
            for k in range(i, maps):
                total = acc_ref[pair, :, cols]
                for x in spectra_rows:
                    total = total + x[i] * x[k] + x[maps + i] * x[maps + k]
                acc_ref[pair, :, cols] = total
                pair += 1
        return 0

    lax.fori_loop(0, blocks, project, 0)

    @pl.when(step == pl.num_programs(0) - 1)
    def _():
        share = cross_ref.shape[2]

        def finish(d, _):
            for part in range(share // LBLK):
                cols = pl.ds(pl.multiple_of(d * share + part * LBLK, LBLK), LBLK)
                cross_ref[d, : acc_ref.shape[0], part * LBLK : (part + 1) * LBLK] = jnp.sum(
                    acc_ref[:, :, cols], axis=1
                ).astype(cross_ref.dtype)
            return 0

        lax.fori_loop(0, cross_ref.shape[0], finish, 0)


def project_blocks(legendre_starts, heights, m_float, first_l, modes, maps_count, cycle_scale, blk_total):
    local_cols, block_count, cycles = legendre_starts.shape[1:]
    local_len = block_count * LBLK
    q_group = KDIM // cycles
    parts = 2 * maps_count
    pairs = maps_count * (maps_count + 1) // 2
    base_l = first_l.astype(jnp.float32) + LBLK * jnp.arange(block_count, dtype=jnp.float32)
    degree = base_l[None, :] - 1.0
    m_col = m_float[:, None]
    coef = jnp.sqrt((4.0 * degree * degree - 1.0) / ((degree - m_col) * (degree + m_col)))
    starts = jnp.stack([legendre_starts[0] / coef[:, :, None], legendre_starts[1]])
    starts = jnp.transpose(starts, (0, 2, 1, 3)).reshape(2, block_count, local_cols * cycles)
    z_row = jnp.tile(heights, STEP_LANES // cycles)[None]
    m_row = jnp.tile(m_float, 256 // local_cols)[None]
    base = jnp.broadcast_to(base_l[:, None], (block_count, 256))
    groups = STEP_LANES // KDIM
    step_cols = groups * q_group
    dims = (block_count, cycles, maps_count, q_group, cycle_scale)
    pair_rows = -(-pairs // 16) * 16
    share = local_len // blk_total
    whole = lambda shape: pl.BlockSpec(shape, lambda i: (0,) * len(shape))
    return pl.pallas_call(
        functools.partial(spectra_kernel, dims),
        grid=(local_cols // step_cols,),
        out_shape=(
            jax.ShapeDtypeStruct((parts, local_cols, local_len), jnp.bfloat16),
            jax.ShapeDtypeStruct((blk_total, pair_rows, share), jnp.bfloat16),
        ),
        in_specs=[
            pl.BlockSpec((2, block_count, STEP_LANES), lambda i: (0, 0, i)),
            whole((1, STEP_LANES)),
            whole((1, 256)),
            whole((block_count, 256)),
            pl.BlockSpec((step_cols // MGRP, cycles, 128), lambda i: (i, 0, 0)),
        ],
        out_specs=(
            pl.BlockSpec((parts, step_cols, local_len), lambda i: (0, i, 0)),
            whole((blk_total, pair_rows, share)),
        ),
        scratch_shapes=[
            pltpu.VMEM((block_count * (LBLK + GAP), 128), jnp.float32),
            pltpu.VMEM((block_count, 128, LBLK), jnp.float32),
            pltpu.VMEM((local_len, 256), jnp.bfloat16),
            pltpu.VMEM((local_len, STEP_LANES), jnp.float32),
            pltpu.VMEM((STEP_LANES // 128, block_count * (LBLK + GAP), 128), jnp.float32),
            pltpu.VMEM((pairs, 8, local_len), jnp.float32),
        ],
        compiler_params=pltpu.CompilerParams(vmem_limit_bytes=60 * 1024 * 1024),
    )(starts, z_row, m_row, base, modes)


def modes_kernel(totals, sky_ref, first_ref, wr_ref, wi_ref, phase_ref, out_ref,
                 rows_ref, turned_ref, held_ref, send_sem, recv_sem):
    blk_total, map_total, factor = totals
    maps = sky_ref.shape[0]
    count = blk_total * map_total
    me_blk, me_map = lax.axis_index("blk"), lax.axis_index("map")
    me = me_blk * map_total + me_map
    share = RES // blk_total
    barrier = pltpu.get_barrier_semaphore()
    for i in range(1, count):
        peer = lax.rem(me + i, count)
        pl.semaphore_signal(
            barrier, inc=1,
            device_id={"blk": peer // map_total, "map": lax.rem(peer, map_total)},
            device_id_type=pl.DeviceIdType.MESH,
        )
    rows_ref[...] = jnp.zeros_like(rows_ref)
    first = first_ref[...]
    for n in range(maps):
        section = lax.dot_general(
            sky_ref[n], first, (((0,), (0,)), ((), ())), preferred_element_type=jnp.float32
        )
        section = section.astype(jnp.bfloat16).astype(jnp.float32)
        part_re, part_im = section[:, :RES], section[:, RES:]
        for c in range(MGRP):
            wave_re = wr_ref[c].astype(jnp.float32)
            wave_im = wi_ref[c].astype(jnp.float32)
            real = jnp.sum(wave_re * part_re - wave_im * part_im, axis=0, keepdims=True)
            imag = jnp.sum(wave_re * part_im + wave_im * part_re, axis=0, keepdims=True)
            cos, sin = phase_ref[c : c + 1], phase_ref[MGRP + c : MGRP + c + 1]
            row = c * 2 * maps + n
            rows_ref[row : row + 1, :] = factor * (cos * real + sin * imag)
            rows_ref[row + maps : row + maps + 1, :] = factor * (cos * imag - sin * real)
    turned_ref[...] = rows_ref[...].T.astype(jnp.bfloat16)
    pl.semaphore_wait(barrier, count - 1)

    def copy_to(peer, source):
        target_blk = peer // map_total
        return pltpu.make_async_remote_copy(
            src_ref=turned_ref.at[pl.ds(pl.multiple_of(target_blk * share, share), share)],
            dst_ref=held_ref.at[source],
            send_sem=send_sem.at[peer],
            recv_sem=recv_sem.at[source],
            device_id={"blk": target_blk, "map": lax.rem(peer, map_total)},
            device_id_type=pl.DeviceIdType.MESH,
        )

    for i in range(1, count):
        copy_to(lax.rem(me + i, count), me).start()
    held_ref[me] = turned_ref[pl.ds(pl.multiple_of(me_blk * share, share), share), :]
    for i in range(1, count):
        peer = lax.rem(me + i, count)
        copy_to(peer, peer).wait_recv()
    for i in range(1, count):
        copy_to(lax.rem(me + i, count), me).wait_send()
    gathered = held_ref[...].astype(jnp.float32)
    out_ref[...] = jnp.swapaxes(gathered, 0, 1).astype(jnp.bfloat16)


def exchange_modes(sky_maps, parity, blk_total, map_total):
    _, maps, cycle_len = sky_maps.shape
    first_table, wave_re, wave_im = constant_tables(cycle_len)
    m_value = MSTART + np.arange(MGRP)[:, None] * RES + np.arange(RES)[None, :]
    m_value = jnp.asarray(m_value, jnp.int32)
    angle = math.pi / cycle_len * (m_value * parity[0] % (2 * cycle_len)).astype(jnp.float32)
    phase = jnp.concatenate([jnp.cos(angle), jnp.sin(angle)], axis=0)
    count = blk_total * map_total
    return pl.pallas_call(
        functools.partial(modes_kernel, (blk_total, map_total, 1.0 / math.sqrt(cycle_len))),
        out_shape=jax.ShapeDtypeStruct((RES // blk_total, count, 128), jnp.bfloat16),
        in_specs=[pl.BlockSpec(memory_space=pltpu.VMEM)] * 5,
        out_specs=pl.BlockSpec(memory_space=pltpu.VMEM),
        scratch_shapes=[
            pltpu.VMEM((128, RES), jnp.float32),
            pltpu.VMEM((RES, 128), jnp.bfloat16),
            pltpu.VMEM((count, RES // blk_total, 128), jnp.bfloat16),
            pltpu.SemaphoreType.DMA((count,)),
            pltpu.SemaphoreType.DMA((count,)),
        ],
        compiler_params=pltpu.CompilerParams(collective_id=0, has_side_effects=True),
    )(sky_maps.reshape(maps, RES, cycle_len // RES), first_table, wave_re, wave_im, phase)


def constant_tables(cycle_len):
    low_len = cycle_len // RES
    residue = np.arange(RES)
    angle = np.float32(2.0 * math.pi / RES) * (
        residue[:, None] * residue[None, :] % RES
    ).astype(np.float32)
    first = np.concatenate([np.cos(angle), -np.sin(angle)], axis=1)
    m_value = MSTART + RES * np.arange(MGRP)[:, None, None] + residue[None, None, :]
    turn = m_value * np.arange(low_len)[None, :, None] % cycle_len
    angle = np.float32(2.0 * math.pi / cycle_len) * turn.astype(np.float32)
    short = lambda table: jnp.asarray(table.astype(jnp.bfloat16))
    return short(first), short(np.cos(angle)), short(-np.sin(angle))


def total_kernel(blk_total, maps, part_ref, out_ref, held_ref, send_sem, recv_sem):
    me = lax.axis_index("blk")
    barrier = pltpu.get_barrier_semaphore()
    for i in range(1, blk_total):
        pl.semaphore_signal(
            barrier, inc=1, device_id={"blk": lax.rem(me + i, blk_total)},
            device_id_type=pl.DeviceIdType.MESH,
        )
    pl.semaphore_wait(barrier, blk_total - 1)

    def copy_to(peer, source):
        return pltpu.make_async_remote_copy(
            src_ref=part_ref.at[peer],
            dst_ref=held_ref.at[source],
            send_sem=send_sem.at[peer],
            recv_sem=recv_sem.at[source],
            device_id={"blk": peer},
            device_id_type=pl.DeviceIdType.MESH,
        )

    order = [lax.rem(me + i, blk_total) for i in range(1, blk_total)]
    for peer in order:
        copy_to(peer, me).start()
    total = part_ref[me].astype(jnp.float32)
    for peer in order:
        copy_to(peer, peer).wait_recv()
        total = total + held_ref[peer].astype(jnp.float32)
    total = total * (1.0 / (MGRP * RES))
    pair = 0
    for i in range(maps):
        for k in range(i, maps):
            out_ref[i, k : k + 1, :] = total[pair : pair + 1]
            if k > i:
                out_ref[k, i : i + 1, :] = total[pair : pair + 1]
            pair += 1
    for peer in order:
        copy_to(peer, me).wait_send()


def total_cross(cross, maps):
    blk_total, pair_rows, share = cross.shape
    return pl.pallas_call(
        functools.partial(total_kernel, blk_total, maps),
        out_shape=jax.ShapeDtypeStruct((maps, maps, share), jnp.float32),
        in_specs=[pl.BlockSpec(memory_space=pltpu.VMEM)],
        out_specs=pl.BlockSpec(memory_space=pltpu.VMEM),
        scratch_shapes=[
            pltpu.VMEM(cross.shape, cross.dtype),
            pltpu.SemaphoreType.DMA((blk_total,)),
            pltpu.SemaphoreType.DMA((blk_total,)),
        ],
        compiler_params=pltpu.CompilerParams(collective_id=1, has_side_effects=True),
    )(cross)


def kernel_fits(own_cycles, blk_total, cycles, maps_count, block_count):
    local_cols = MGRP * RES // blk_total
    return (
        own_cycles == 1
        and local_cols == 64
        and KDIM % cycles == 0
        and KDIM // cycles == 8
        and 2 * maps_count * MGRP <= 128
        and block_count % 8 == 0
        and block_count % blk_total == 0
    )


def fast_body(sky_maps, cycle_number, legendre_starts):
    _, maps_count, _ = sky_maps.shape
    map_total = lax.axis_size("map")
    blk_total = lax.axis_size("blk")
    row = lax.axis_index("blk") * map_total + lax.axis_index("map")
    parity = (lax.dynamic_slice_in_dim(cycle_number, row, 1) - NSIDE + 1) % 2
    modes = exchange_modes(sky_maps, parity, blk_total, map_total)
    heights = cycle_height(cycle_number)
    local_cols, block_count, cycles = legendre_starts.shape[1:]
    column = lax.axis_index("blk") * local_cols + jnp.arange(local_cols, dtype=jnp.int32)
    m_float = (MSTART + RES * (column % MGRP) + column // MGRP).astype(jnp.float32)
    first_l = LSTART + lax.axis_index("map") * block_count * LBLK
    cycle_scale = 1.0 / math.sqrt(cycles)
    harmonics, cross = project_blocks(
        legendre_starts, heights, m_float, first_l, modes, maps_count, cycle_scale, blk_total
    )
    spectra = total_cross(cross, maps_count)
    return (jnp.transpose(harmonics, (1, 0, 2)), spectra[None])


def body(sky_maps, cycle_number, legendre_starts):
    own_cycles, maps_count, cycle_len = sky_maps.shape
    map_total = lax.axis_size("map")
    blk_total = lax.axis_size("blk")
    cycles, block_count = cycle_number.shape[0], legendre_starts.shape[2]
    if kernel_fits(own_cycles, blk_total, cycles, maps_count, block_count):
        return fast_body(sky_maps, cycle_number, legendre_starts)
    tables = dft_tables(cycle_len)
    first_row = (lax.axis_index("blk") * map_total + lax.axis_index("map")) * own_cycles
    own_numbers = lax.dynamic_slice_in_dim(cycle_number, first_row, own_cycles)
    parity = (own_numbers - NSIDE + 1) % 2
    local_modes = cycle_transform(sky_maps, parity, tables)
    grouped = lax.all_gather(local_modes, "map", axis=0, tiled=True)
    regrouped = lax.all_to_all(grouped, "blk", split_axis=4, concat_axis=0, tiled=True)
    ordered = jnp.transpose(regrouped, (4, 3, 1, 2, 0))
    local_cols = ordered.shape[0] * ordered.shape[1]
    cycle_modes = ordered.reshape(local_cols, 2 * maps_count, -1)
    heights = cycle_height(cycle_number)
    column = lax.axis_index("blk") * local_cols + jnp.arange(local_cols, dtype=jnp.int32)
    m_float = (MSTART + RES * (column % MGRP) + column // MGRP).astype(jnp.float32)
    block_count = legendre_starts.shape[2]
    local_len = block_count * LBLK
    first_l = LSTART + lax.axis_index("map") * local_len
    cycle_scale = 1.0 / math.sqrt(cycle_modes.shape[-1])

    def one_block(block_index):
        start_pair = lax.dynamic_index_in_dim(legendre_starts, block_index, 2, keepdims=False)
        legendre_tile = legendre_rows(
            start_pair, heights, m_float, first_l + block_index * LBLK
        ).astype(jnp.bfloat16)
        projected = (
            jnp.einsum(
                "qlr,qnr->qnl", legendre_tile, cycle_modes, preferred_element_type=jnp.float32
            )
            * cycle_scale
        )
        return projected.astype(jnp.bfloat16)

    blocks_out = lax.map(one_block, jnp.arange(block_count, dtype=jnp.int32))
    harmonics = jnp.transpose(blocks_out, (1, 2, 0, 3)).reshape(
        local_cols, 2 * maps_count, local_len
    )
    total_cols = MGRP * RES
    spread = harmonics.reshape(local_cols, 2 * maps_count, blk_total, local_len // blk_total)
    spread = jnp.transpose(spread, (2, 3, 1, 0))
    received = lax.all_to_all(
        shortened(spread), "blk", split_axis=0, concat_axis=3, tiled=True
    ).astype(spread.dtype)
    item_count = received.shape[1]
    split_piece = received.reshape(item_count, 2, maps_count, received.shape[3])
    cross_sum = jnp.einsum(
        "gciq,gcjq->ijg", split_piece, split_piece, preferred_element_type=jnp.float32
    )
    owned = (cross_sum / total_cols)[None]
    return (harmonics, owned)


def solution(mesh):
    return jax.shard_map(
        body,
        mesh=mesh,
        in_specs=(P(("blk", "map"), None, None), P(), P(None, "blk", "map", None)),
        out_specs=(P("blk", None, "map"), P("map", None, None, "blk")),
        check_vma=False,
    )
```

```python
import functools
import math

import jax
import jax.numpy as jnp
import numpy as np
from jax import lax
from jax.experimental import pallas as pl
from jax.experimental.pallas import tpu as pltpu
from jax.sharding import PartitionSpec as P

NSIDE = 8192
RES = 128
MGRP = 4
MSTART = 4096
LSTART = 8192
LBLK = 128


def shortened(array):

    def short(part):
        return part.astype(jnp.bfloat16) if part.dtype == jnp.float32 else part

    return jax.tree.map(short, array)


def cycle_height(cycle_ids):
    return (4.0 * NSIDE - 2.0 * cycle_ids.astype(jnp.float32)) / (3.0 * NSIDE)


def dft_tables(cycle_len):
    low_len = cycle_len // RES
    residue = jnp.arange(RES, dtype=jnp.int32)
    turn_one = residue[:, None] * residue[None, :] % RES
    angle_one = 2.0 * math.pi / RES * turn_one.astype(jnp.float32)
    first_table = jnp.concatenate([jnp.cos(angle_one), -jnp.sin(angle_one)], axis=1).astype(
        jnp.bfloat16
    )
    column_group = jnp.arange(MGRP, dtype=jnp.int32)
    sample = jnp.arange(low_len, dtype=jnp.int32)
    m_value = MSTART + RES * column_group[:, None, None] + residue[None, None, :]
    turn_two = m_value * sample[None, :, None] % cycle_len
    angle_two = 2.0 * math.pi / cycle_len * turn_two.astype(jnp.float32)
    twiddle_re = jnp.cos(angle_two).astype(jnp.bfloat16)
    twiddle_im = (-jnp.sin(angle_two)).astype(jnp.bfloat16)
    return (first_table, twiddle_re, twiddle_im)


def cycle_transform(cycle_rows, parity, tables):
    first_table, twiddle_re, twiddle_im = tables
    cycle_count, maps_count, cycle_len = cycle_rows.shape
    low_len = cycle_len // RES
    folded = cycle_rows.reshape(cycle_count, maps_count, RES, low_len)
    section_one = jnp.einsum(
        "rnaj,ak->rnjk", folded, first_table, preferred_element_type=jnp.float32
    )
    section_one = section_one.astype(jnp.bfloat16)
    part_re = section_one[..., :RES]
    part_im = section_one[..., RES:]
    real_sum = jnp.einsum(
        "rnjk,cjk->rnck", part_re, twiddle_re, preferred_element_type=jnp.float32
    ) - jnp.einsum("rnjk,cjk->rnck", part_im, twiddle_im, preferred_element_type=jnp.float32)
    imag_sum = jnp.einsum(
        "rnjk,cjk->rnck", part_im, twiddle_re, preferred_element_type=jnp.float32
    ) + jnp.einsum("rnjk,cjk->rnck", part_re, twiddle_im, preferred_element_type=jnp.float32)
    column_group = jnp.arange(MGRP, dtype=jnp.int32)
    residue = jnp.arange(RES, dtype=jnp.int32)
    m_value = MSTART + RES * column_group[:, None] + residue[None, :]
    shifted = m_value[None, :, :] * parity[:, None, None] % (2 * cycle_len)
    phase_angle = math.pi / cycle_len * shifted.astype(jnp.float32)
    cos_part = jnp.cos(phase_angle)[:, None]
    sin_part = jnp.sin(phase_angle)[:, None]
    factor = 1.0 / math.sqrt(cycle_len)
    out_re = factor * (cos_part * real_sum + sin_part * imag_sum)
    out_im = factor * (cos_part * imag_sum - sin_part * real_sum)
    return jnp.stack([out_re, out_im], axis=1).astype(jnp.bfloat16)


def legendre_rows(start_pair, height, m_float, first_l):
    m_column = m_float[:, None]

    def recur_coef(degree):
        return jnp.sqrt((4.0 * degree * degree - 1.0) / ((degree - m_column) * (degree + m_column)))

    base_l = first_l.astype(jnp.float32)
    value_older = start_pair[0]
    value_newer = start_pair[1]
    prior_coef = recur_coef(base_l - 1.0)
    height_row = height[None, :]
    stacked_rows = []
    for offset in range(LBLK):
        present_coef = recur_coef(base_l + offset)
        value_now = present_coef * (height_row * value_newer - value_older / prior_coef)
        stacked_rows.append(value_now)
        value_older = value_newer
        value_newer = value_now
        prior_coef = present_coef
    return jnp.stack(stacked_rows, axis=1)


STEP_LANES = 1024
KDIM = 256
GAP = 8


def spectra_kernel(
    dims, starts_ref, z_ref, turned_ref, pieces_ref, modes_ref, harm_ref, cross_ref,
    leg_ref, acc_ref,
):
    blocks, cycles, maps, q_group, scale = dims
    step = pl.program_id(0)
    groups = STEP_LANES // KDIM
    halves = STEP_LANES // 128
    parts = 2 * maps

    @pl.when(step == 0)
    def _():
        acc_ref[...] = jnp.zeros_like(acc_ref)

    q_row = lax.broadcasted_iota(jnp.int32, (256, STEP_LANES), 0)
    q_lane = lax.broadcasted_iota(jnp.int32, (256, STEP_LANES), 1) // cycles + step * (
        STEP_LANES // cycles
    )
    spread = jnp.where((q_row % 64 == q_lane) & (q_row < 192), 1.0, 0.0).astype(jnp.bfloat16)

    run = 16

    def recur(i, carry):
        older, newer = carry
        rows = pl.ds(pl.multiple_of(i * run * blocks, run * blocks), run * blocks)
        kap = jnp.dot(pieces_ref[rows, :], spread, preferred_element_type=jnp.float32)
        for j in range(run):
            now = (kap[j * blocks : (j + 1) * blocks] * z_ref[...]) * newer - older
            for half in range(blocks // 8):
                at = pl.ds(half * 8 * (LBLK + GAP) + i * run + j, 8, stride=LBLK + GAP)
                for g in range(halves):
                    leg_ref[g, at, :] = now[half * 8 : half * 8 + 8, g * 128 : g * 128 + 128]
            older, newer = newer, now
        return older, newer

    lax.fori_loop(0, LBLK // run, recur, (starts_ref[0], starts_ref[1]))

    rows_all = parts * q_group
    row = lax.broadcasted_iota(jnp.int32, (rows_all, 128), 0)
    lane = lax.broadcasted_iota(jnp.int32, (rows_all, 128), 1)
    picked = (row % MGRP) * parts + row // q_group == lane
    row = lax.broadcasted_iota(jnp.int32, (rows_all, KDIM), 0)
    lane = lax.broadcasted_iota(jnp.int32, (rows_all, KDIM), 1)
    same_q = row % q_group == lane // cycles
    cyc = lax.broadcasted_iota(jnp.int32, (cycles, KDIM), 0)
    lane_c = lax.broadcasted_iota(jnp.int32, (cycles, KDIM), 1) % cycles
    tile = jnp.where(cyc == lane_c, 1.0, 0.0).astype(jnp.bfloat16)
    row_k = lax.broadcasted_iota(jnp.int32, (rows_all, 128), 0) % q_group // MGRP
    per_group = q_group // MGRP
    weights = []
    for g in range(groups):
        narrow = jnp.zeros((rows_all, cycles), jnp.float32)
        for k in range(per_group):
            pick = jnp.where(picked & (row_k == k), 1.0, 0.0).astype(jnp.bfloat16)
            narrow = narrow + lax.dot_general(
                pick, modes_ref[g * per_group + k], (((1,), (1,)), ((), ())),
                preferred_element_type=jnp.float32,
            )
        wide = jnp.dot(narrow.astype(jnp.bfloat16), tile, preferred_element_type=jnp.float32)
        weights.append(jnp.where(same_q, wide, 0.0).astype(jnp.bfloat16))

    def project(u, _):
        cols = pl.ds(pl.multiple_of(u * 2 * LBLK, 2 * LBLK), 2 * LBLK)
        sources = [
            pl.ds(pl.multiple_of((2 * u + x) * (LBLK + GAP), 8), LBLK) for x in range(2)
        ]
        spectra_rows = []
        for g in range(groups):
            first = pl.multiple_of((step * groups + g) * q_group, 8)
            p_rows = jnp.concatenate(
                [turned_ref[2 * u + x, pl.ds(first, q_group), :] for x in range(2)], axis=1
            ) * scale
            leg = jnp.concatenate(
                [
                    jnp.concatenate(
                        [leg_ref[g * (KDIM // 128) + h, src, :] for h in range(KDIM // 128)],
                        axis=1,
                    )
                    for src in sources
                ],
                axis=0,
            ).astype(jnp.bfloat16)
            out = lax.dot_general(
                weights[g], leg, (((1,), (1,)), ((), ())), preferred_element_type=jnp.float32
            )
            crossed = out.reshape(parts, q_group, 2 * LBLK) * p_rows[None]
            crossed = crossed.astype(jnp.bfloat16)
            harm_ref[:, g * q_group : (g + 1) * q_group, cols] = crossed
            spectra_rows.append(crossed.astype(jnp.float32))
        pair = 0
        for i in range(maps):
            for k in range(i, maps):
                total = acc_ref[pair, :, cols]
                for x in spectra_rows:
                    total = total + x[i] * x[k] + x[maps + i] * x[maps + k]
                acc_ref[pair, :, cols] = total
                pair += 1
        return 0

    lax.fori_loop(0, blocks // 2, project, 0)

    @pl.when(step == pl.num_programs(0) - 1)
    def _():
        share = cross_ref.shape[2]

        def finish(d, _):
            for part in range(share // LBLK):
                cols = pl.ds(pl.multiple_of(d * share + part * LBLK, LBLK), LBLK)
                cross_ref[d, : acc_ref.shape[0], part * LBLK : (part + 1) * LBLK] = jnp.sum(
                    acc_ref[:, :, cols], axis=1
                ).astype(cross_ref.dtype)
            return 0

        lax.fori_loop(0, cross_ref.shape[0], finish, 0)


def project_blocks(
    legendre_starts, m_float, first_l, prepared, maps_count, cycle_scale, blk_total
):
    modes, pieces, turned, z_row = prepared
    local_cols, block_count, cycles = legendre_starts.shape[1:]
    local_len = block_count * LBLK
    q_group = KDIM // cycles
    parts = 2 * maps_count
    pairs = maps_count * (maps_count + 1) // 2
    base_l = first_l.astype(jnp.float32) + LBLK * jnp.arange(block_count, dtype=jnp.float32)
    degree = base_l[None, :] - 1.0
    m_col = m_float[:, None]
    coef = jnp.sqrt((4.0 * degree * degree - 1.0) / ((degree - m_col) * (degree + m_col)))
    starts = jnp.stack([legendre_starts[0] / coef[:, :, None], legendre_starts[1]])
    starts = jnp.transpose(starts, (0, 2, 1, 3)).reshape(2, block_count, local_cols * cycles)
    groups = STEP_LANES // KDIM
    step_cols = groups * q_group
    dims = (block_count, cycles, maps_count, q_group, cycle_scale)
    pair_rows = -(-pairs // 16) * 16
    share = local_len // blk_total
    whole = lambda shape: pl.BlockSpec(shape, lambda i: (0,) * len(shape))
    return pl.pallas_call(
        functools.partial(spectra_kernel, dims),
        grid=(local_cols // step_cols,),
        out_shape=(
            jax.ShapeDtypeStruct((parts, local_cols, local_len), jnp.bfloat16),
            jax.ShapeDtypeStruct((blk_total, pair_rows, share), jnp.bfloat16),
        ),
        in_specs=[
            pl.BlockSpec((2, block_count, STEP_LANES), lambda i: (0, 0, i)),
            whole((1, STEP_LANES)),
            whole(turned.shape),
            whole(pieces.shape),
            pl.BlockSpec((step_cols // MGRP, cycles, 128), lambda i: (i, 0, 0)),
        ],
        out_specs=(
            pl.BlockSpec((parts, step_cols, local_len), lambda i: (0, i, 0)),
            whole((blk_total, pair_rows, share)),
        ),
        scratch_shapes=[
            pltpu.VMEM((STEP_LANES // 128, block_count * (LBLK + GAP), 128), jnp.float32),
            pltpu.VMEM((pairs, 8, local_len), jnp.float32),
        ],
        compiler_params=pltpu.CompilerParams(vmem_limit_bytes=60 * 1024 * 1024),
    )(starts, z_row, turned, pieces, modes)


def modes_kernel(
    totals, number_ref, sky_ref, first_ref, wr_ref, wi_ref, phase_ref,
    out_ref, pieces_ref, scales_ref, z_ref, rows_ref, turned_ref, held_ref, p_ref,
    send_sem, recv_sem,
):
    blk_total, map_total, factor = totals
    maps = sky_ref.shape[0]
    count = blk_total * map_total
    me_blk, me_map = lax.axis_index("blk"), lax.axis_index("map")
    me = me_blk * map_total + me_map
    share = RES // blk_total
    barrier = pltpu.get_barrier_semaphore()
    for i in range(1, count):
        peer = lax.rem(me + i, count)
        pl.semaphore_signal(
            barrier, inc=1,
            device_id={"blk": peer // map_total, "map": lax.rem(peer, map_total)},
            device_id_type=pl.DeviceIdType.MESH,
        )
    rows_ref[...] = jnp.zeros_like(rows_ref)
    first = first_ref[...]
    parity = (number_ref[me] - NSIDE + 1) % 2
    odd = jnp.full((MGRP, RES), parity, jnp.int32) == 1
    cosines = jnp.where(odd, phase_ref[:MGRP], 1.0)
    sines = jnp.where(odd, phase_ref[MGRP:], 0.0)
    for n in range(maps):
        section = lax.dot_general(
            sky_ref[n], first, (((0,), (0,)), ((), ())), preferred_element_type=jnp.float32
        )
        section = section.astype(jnp.bfloat16).astype(jnp.float32)
        part_re, part_im = section[:, :RES], section[:, RES:]
        for c in range(MGRP):
            wave_re = wr_ref[c].astype(jnp.float32)
            wave_im = wi_ref[c].astype(jnp.float32)
            real = jnp.sum(wave_re * part_re - wave_im * part_im, axis=0, keepdims=True)
            imag = jnp.sum(wave_re * part_im + wave_im * part_re, axis=0, keepdims=True)
            cos, sin = cosines[c : c + 1], sines[c : c + 1]
            row = c * 2 * maps + n
            rows_ref[row : row + 1, :] = factor * (cos * real + sin * imag)
            rows_ref[row + maps : row + maps + 1, :] = factor * (cos * imag - sin * real)
    turned_ref[...] = rows_ref[...].T.astype(jnp.bfloat16)
    pl.semaphore_wait(barrier, count - 1)

    def copy_to(peer, source):
        target_blk = peer // map_total
        return pltpu.make_async_remote_copy(
            src_ref=turned_ref.at[pl.ds(pl.multiple_of(target_blk * share, share), share)],
            dst_ref=held_ref.at[source],
            send_sem=send_sem.at[peer],
            recv_sem=recv_sem.at[source],
            device_id={"blk": target_blk, "map": lax.rem(peer, map_total)},
            device_id_type=pl.DeviceIdType.MESH,
        )

    for i in range(1, count):
        copy_to(lax.rem(me + i, count), me).start()
    held_ref[me] = turned_ref[pl.ds(pl.multiple_of(me_blk * share, share), share), :]
    prepare(blk_total, number_ref, pieces_ref, scales_ref, z_ref, p_ref)
    for i in range(1, count):
        peer = lax.rem(me + i, count)
        copy_to(peer, peer).wait_recv()
    for i in range(1, count):
        copy_to(lax.rem(me + i, count), me).wait_send()
    gathered = held_ref[...].astype(jnp.float32)
    out_ref[...] = jnp.swapaxes(gathered, 0, 1).astype(jnp.bfloat16)


def prepare(blk_total, number_ref, pieces_ref, scales_ref, z_ref, p_ref):
    blocks = scales_ref.shape[0]
    local_cols = MGRP * RES // blk_total
    lane = lax.broadcasted_iota(jnp.int32, z_ref.shape, 1) % number_ref.shape[0]
    numbers = jnp.zeros(z_ref.shape, jnp.int32)
    for r in range(number_ref.shape[0]):
        numbers = jnp.where(lane == r, number_ref[r], numbers)
    z_ref[...] = cycle_height(numbers)
    lane = lax.broadcasted_iota(jnp.int32, (blocks, 256), 1)
    piece = lane // local_cols
    column = lax.axis_index("blk") * local_cols + lane % local_cols
    m_row = (MSTART + RES * (column % MGRP) + column // MGRP).astype(jnp.float32)
    block = lax.broadcasted_iota(jnp.int32, (blocks, 256), 0)
    base = LSTART + (lax.axis_index("map") * blocks + block) * LBLK

    def setup(j, carry):
        p_prev, q_prev = carry
        degree = (base + j).astype(jnp.float32)
        num = 4.0 * degree * degree - 1.0
        den = (degree - m_row) * (degree + m_row)
        root = lax.rsqrt(num * den)
        kappa = p_prev * p_prev
        high = kappa.astype(jnp.bfloat16).astype(jnp.float32)
        rest = kappa - high
        mid = rest.astype(jnp.bfloat16).astype(jnp.float32)
        low = rest - mid
        pieces = jnp.where(piece == 0, high, jnp.where(piece == 1, mid, low))
        pieces_ref[pl.ds(pl.multiple_of(j * blocks, blocks), blocks), :] = pieces.astype(
            jnp.bfloat16
        )
        p_now = num * root * q_prev
        q_now = den * root * p_prev
        for half in range(blocks // 8):
            p_ref[pl.ds(half * 8 * (LBLK + GAP) + j, 8, stride=LBLK + GAP), :] = p_now[
                half * 8 : half * 8 + 8, :128
            ]
        return p_now, q_now

    one = jnp.ones((blocks, 256), jnp.float32)
    lax.fori_loop(0, LBLK, setup, (one, one), unroll=4)

    def turn(t, _):
        turned = p_ref[pl.ds(pl.multiple_of(t * (LBLK + GAP), 8), LBLK), :].T
        scales_ref[t] = turned[:local_cols]
        return 0

    lax.fori_loop(0, blocks, turn, 0)


def exchange_modes(sky_maps, cycle_number, block_count, blk_total, map_total):
    _, maps, cycle_len = sky_maps.shape
    first_table, wave_re, wave_im = constant_tables(cycle_len)
    m_value = MSTART + np.arange(MGRP)[:, None] * RES + np.arange(RES)[None, :]
    angle = np.float32(math.pi / cycle_len) * (m_value % (2 * cycle_len)).astype(np.float32)
    phase = jnp.asarray(np.concatenate([np.cos(angle), np.sin(angle)], axis=0))
    count = blk_total * map_total
    return pl.pallas_call(
        functools.partial(modes_kernel, (blk_total, map_total, 1.0 / math.sqrt(cycle_len))),
        out_shape=(
            jax.ShapeDtypeStruct((RES // blk_total, count, 128), jnp.bfloat16),
            jax.ShapeDtypeStruct((block_count * LBLK, 256), jnp.bfloat16),
            jax.ShapeDtypeStruct((block_count, MGRP * RES // blk_total, LBLK), jnp.float32),
            jax.ShapeDtypeStruct((1, STEP_LANES), jnp.float32),
        ),
        in_specs=[pl.BlockSpec(memory_space=pltpu.SMEM)]
        + [pl.BlockSpec(memory_space=pltpu.VMEM)] * 5,
        out_specs=(pl.BlockSpec(memory_space=pltpu.VMEM),) * 4,
        scratch_shapes=[
            pltpu.VMEM((128, RES), jnp.float32),
            pltpu.VMEM((RES, 128), jnp.bfloat16),
            pltpu.VMEM((count, RES // blk_total, 128), jnp.bfloat16),
            pltpu.VMEM((block_count * (LBLK + GAP), 128), jnp.float32),
            pltpu.SemaphoreType.DMA((count,)),
            pltpu.SemaphoreType.DMA((count,)),
        ],
        compiler_params=pltpu.CompilerParams(collective_id=0, has_side_effects=True),
    )(cycle_number, sky_maps.reshape(maps, RES, cycle_len // RES), first_table, wave_re, wave_im, phase)


def constant_tables(cycle_len):
    low_len = cycle_len // RES
    residue = np.arange(RES)
    angle = np.float32(2.0 * math.pi / RES) * (
        residue[:, None] * residue[None, :] % RES
    ).astype(np.float32)
    first = np.concatenate([np.cos(angle), -np.sin(angle)], axis=1)
    m_value = MSTART + RES * np.arange(MGRP)[:, None, None] + residue[None, None, :]
    turn = m_value * np.arange(low_len)[None, :, None] % cycle_len
    angle = np.float32(2.0 * math.pi / cycle_len) * turn.astype(np.float32)
    short = lambda table: jnp.asarray(table.astype(jnp.bfloat16))
    return short(first), short(np.cos(angle)), short(-np.sin(angle))


def total_kernel(blk_total, maps, part_ref, out_ref, held_ref, send_sem, recv_sem):
    me = lax.axis_index("blk")
    barrier = pltpu.get_barrier_semaphore()
    for i in range(1, blk_total):
        pl.semaphore_signal(
            barrier, inc=1, device_id={"blk": lax.rem(me + i, blk_total)},
            device_id_type=pl.DeviceIdType.MESH,
        )
    pl.semaphore_wait(barrier, blk_total - 1)

    def copy_to(peer, source):
        return pltpu.make_async_remote_copy(
            src_ref=part_ref.at[peer],
            dst_ref=held_ref.at[source],
            send_sem=send_sem.at[peer],
            recv_sem=recv_sem.at[source],
            device_id={"blk": peer},
            device_id_type=pl.DeviceIdType.MESH,
        )

    order = [lax.rem(me + i, blk_total) for i in range(1, blk_total)]
    for peer in order:
        copy_to(peer, me).start()
    total = part_ref[me].astype(jnp.float32)
    for peer in order:
        copy_to(peer, peer).wait_recv()
        total = total + held_ref[peer].astype(jnp.float32)
    total = total * (1.0 / (MGRP * RES))
    pair = 0
    for i in range(maps):
        for k in range(i, maps):
            out_ref[i, k] = total[pair : pair + 1]
            if k > i:
                out_ref[k, i] = total[pair : pair + 1]
            pair += 1
    for peer in order:
        copy_to(peer, me).wait_send()


def total_cross(cross, maps):
    blk_total, pair_rows, share = cross.shape
    return pl.pallas_call(
        functools.partial(total_kernel, blk_total, maps),
        out_shape=jax.ShapeDtypeStruct((maps, maps, 1, share), jnp.float32),
        in_specs=[pl.BlockSpec(memory_space=pltpu.VMEM)],
        out_specs=pl.BlockSpec(memory_space=pltpu.VMEM),
        scratch_shapes=[
            pltpu.VMEM(cross.shape, cross.dtype),
            pltpu.SemaphoreType.DMA((blk_total,)),
            pltpu.SemaphoreType.DMA((blk_total,)),
        ],
        compiler_params=pltpu.CompilerParams(collective_id=1, has_side_effects=True),
    )(cross)


def kernel_fits(own_cycles, blk_total, cycles, maps_count, block_count):
    local_cols = MGRP * RES // blk_total
    return (
        own_cycles == 1
        and local_cols == 64
        and KDIM % cycles == 0
        and KDIM // cycles == 8
        and 2 * maps_count * MGRP <= 128
        and block_count % 8 == 0
        and block_count % blk_total == 0
    )


def fast_body(sky_maps, cycle_number, legendre_starts):
    _, maps_count, _ = sky_maps.shape
    map_total = lax.axis_size("map")
    blk_total = lax.axis_size("blk")
    local_cols, block_count, cycles = legendre_starts.shape[1:]
    prepared = exchange_modes(sky_maps, cycle_number, block_count, blk_total, map_total)
    column = lax.axis_index("blk") * local_cols + jnp.arange(local_cols, dtype=jnp.int32)
    m_float = (MSTART + RES * (column % MGRP) + column // MGRP).astype(jnp.float32)
    first_l = LSTART + lax.axis_index("map") * block_count * LBLK
    cycle_scale = 1.0 / math.sqrt(cycles)
    harmonics, cross = project_blocks(
        legendre_starts, m_float, first_l, prepared, maps_count, cycle_scale, blk_total
    )
    spectra = total_cross(cross, maps_count)
    return (jnp.transpose(harmonics, (1, 0, 2)), jnp.transpose(spectra, (2, 0, 1, 3)))


def body(sky_maps, cycle_number, legendre_starts):
    own_cycles, maps_count, cycle_len = sky_maps.shape
    map_total = lax.axis_size("map")
    blk_total = lax.axis_size("blk")
    cycles, block_count = cycle_number.shape[0], legendre_starts.shape[2]
    if kernel_fits(own_cycles, blk_total, cycles, maps_count, block_count):
        return fast_body(sky_maps, cycle_number, legendre_starts)
    tables = dft_tables(cycle_len)
    first_row = (lax.axis_index("blk") * map_total + lax.axis_index("map")) * own_cycles
    own_numbers = lax.dynamic_slice_in_dim(cycle_number, first_row, own_cycles)
    parity = (own_numbers - NSIDE + 1) % 2
    local_modes = cycle_transform(sky_maps, parity, tables)
    grouped = lax.all_gather(local_modes, "map", axis=0, tiled=True)
    regrouped = lax.all_to_all(grouped, "blk", split_axis=4, concat_axis=0, tiled=True)
    ordered = jnp.transpose(regrouped, (4, 3, 1, 2, 0))
    local_cols = ordered.shape[0] * ordered.shape[1]
    cycle_modes = ordered.reshape(local_cols, 2 * maps_count, -1)
    heights = cycle_height(cycle_number)
    column = lax.axis_index("blk") * local_cols + jnp.arange(local_cols, dtype=jnp.int32)
    m_float = (MSTART + RES * (column % MGRP) + column // MGRP).astype(jnp.float32)
    block_count = legendre_starts.shape[2]
    local_len = block_count * LBLK
    first_l = LSTART + lax.axis_index("map") * local_len
    cycle_scale = 1.0 / math.sqrt(cycle_modes.shape[-1])

    def one_block(block_index):
        start_pair = lax.dynamic_index_in_dim(legendre_starts, block_index, 2, keepdims=False)
        legendre_tile = legendre_rows(
            start_pair, heights, m_float, first_l + block_index * LBLK
        ).astype(jnp.bfloat16)
        projected = (
            jnp.einsum(
                "qlr,qnr->qnl", legendre_tile, cycle_modes, preferred_element_type=jnp.float32
            )
            * cycle_scale
        )
        return projected.astype(jnp.bfloat16)

    blocks_out = lax.map(one_block, jnp.arange(block_count, dtype=jnp.int32))
    harmonics = jnp.transpose(blocks_out, (1, 2, 0, 3)).reshape(
        local_cols, 2 * maps_count, local_len
    )
    total_cols = MGRP * RES
    spread = harmonics.reshape(local_cols, 2 * maps_count, blk_total, local_len // blk_total)
    spread = jnp.transpose(spread, (2, 3, 1, 0))
    received = lax.all_to_all(
        shortened(spread), "blk", split_axis=0, concat_axis=3, tiled=True
    ).astype(spread.dtype)
    item_count = received.shape[1]
    split_piece = received.reshape(item_count, 2, maps_count, received.shape[3])
    cross_sum = jnp.einsum(
        "gciq,gcjq->ijg", split_piece, split_piece, preferred_element_type=jnp.float32
    )
    owned = (cross_sum / total_cols)[None]
    return (harmonics, owned)


def solution(mesh):
    return jax.shard_map(
        body,
        mesh=mesh,
        in_specs=(P(("blk", "map"), None, None), P(), P(None, "blk", "map", None)),
        out_specs=(P("blk", None, "map"), P("map", None, None, "blk")),
        check_vma=False,
    )
```

```python
import functools
import math

import jax
import jax.numpy as jnp
import numpy as np
from jax import lax
from jax.experimental import pallas as pl
from jax.experimental.pallas import tpu as pltpu
from jax.sharding import PartitionSpec as P

NSIDE = 8192
RES = 128
MGRP = 4
MSTART = 4096
LSTART = 8192
LBLK = 128


def shortened(array):

    def short(part):
        return part.astype(jnp.bfloat16) if part.dtype == jnp.float32 else part

    return jax.tree.map(short, array)


def cycle_height(cycle_ids):
    return (4.0 * NSIDE - 2.0 * cycle_ids.astype(jnp.float32)) / (3.0 * NSIDE)


def dft_tables(cycle_len):
    low_len = cycle_len // RES
    residue = jnp.arange(RES, dtype=jnp.int32)
    turn_one = residue[:, None] * residue[None, :] % RES
    angle_one = 2.0 * math.pi / RES * turn_one.astype(jnp.float32)
    first_table = jnp.concatenate([jnp.cos(angle_one), -jnp.sin(angle_one)], axis=1).astype(
        jnp.bfloat16
    )
    column_group = jnp.arange(MGRP, dtype=jnp.int32)
    sample = jnp.arange(low_len, dtype=jnp.int32)
    m_value = MSTART + RES * column_group[:, None, None] + residue[None, None, :]
    turn_two = m_value * sample[None, :, None] % cycle_len
    angle_two = 2.0 * math.pi / cycle_len * turn_two.astype(jnp.float32)
    twiddle_re = jnp.cos(angle_two).astype(jnp.bfloat16)
    twiddle_im = (-jnp.sin(angle_two)).astype(jnp.bfloat16)
    return (first_table, twiddle_re, twiddle_im)


def cycle_transform(cycle_rows, parity, tables):
    first_table, twiddle_re, twiddle_im = tables
    cycle_count, maps_count, cycle_len = cycle_rows.shape
    low_len = cycle_len // RES
    folded = cycle_rows.reshape(cycle_count, maps_count, RES, low_len)
    section_one = jnp.einsum(
        "rnaj,ak->rnjk", folded, first_table, preferred_element_type=jnp.float32
    )
    section_one = section_one.astype(jnp.bfloat16)
    part_re = section_one[..., :RES]
    part_im = section_one[..., RES:]
    real_sum = jnp.einsum(
        "rnjk,cjk->rnck", part_re, twiddle_re, preferred_element_type=jnp.float32
    ) - jnp.einsum("rnjk,cjk->rnck", part_im, twiddle_im, preferred_element_type=jnp.float32)
    imag_sum = jnp.einsum(
        "rnjk,cjk->rnck", part_im, twiddle_re, preferred_element_type=jnp.float32
    ) + jnp.einsum("rnjk,cjk->rnck", part_re, twiddle_im, preferred_element_type=jnp.float32)
    column_group = jnp.arange(MGRP, dtype=jnp.int32)
    residue = jnp.arange(RES, dtype=jnp.int32)
    m_value = MSTART + RES * column_group[:, None] + residue[None, :]
    shifted = m_value[None, :, :] * parity[:, None, None] % (2 * cycle_len)
    phase_angle = math.pi / cycle_len * shifted.astype(jnp.float32)
    cos_part = jnp.cos(phase_angle)[:, None]
    sin_part = jnp.sin(phase_angle)[:, None]
    factor = 1.0 / math.sqrt(cycle_len)
    out_re = factor * (cos_part * real_sum + sin_part * imag_sum)
    out_im = factor * (cos_part * imag_sum - sin_part * real_sum)
    return jnp.stack([out_re, out_im], axis=1).astype(jnp.bfloat16)


def legendre_rows(start_pair, height, m_float, first_l):
    m_column = m_float[:, None]

    def recur_coef(degree):
        return jnp.sqrt((4.0 * degree * degree - 1.0) / ((degree - m_column) * (degree + m_column)))

    base_l = first_l.astype(jnp.float32)
    value_older = start_pair[0]
    value_newer = start_pair[1]
    prior_coef = recur_coef(base_l - 1.0)
    height_row = height[None, :]
    stacked_rows = []
    for offset in range(LBLK):
        present_coef = recur_coef(base_l + offset)
        value_now = present_coef * (height_row * value_newer - value_older / prior_coef)
        stacked_rows.append(value_now)
        value_older = value_newer
        value_newer = value_now
        prior_coef = present_coef
    return jnp.stack(stacked_rows, axis=1)


STEP_LANES = 1024
KDIM = 256
GAP = 8


def spectra_kernel(
    dims, starts_ref, z_ref, turned_ref, pieces_ref, modes_ref, harm_ref, cross_ref,
    leg_ref, acc_ref,
):
    blocks, cycles, maps, q_group, scale = dims
    step = pl.program_id(0)
    groups = STEP_LANES // KDIM
    halves = STEP_LANES // 128
    parts = 2 * maps

    @pl.when(step == 0)
    def _():
        acc_ref[...] = jnp.zeros_like(acc_ref)

    q_row = lax.broadcasted_iota(jnp.int32, (256, STEP_LANES), 0)
    q_lane = lax.broadcasted_iota(jnp.int32, (256, STEP_LANES), 1) // cycles + step * (
        STEP_LANES // cycles
    )
    spread = jnp.where((q_row % 64 == q_lane) & (q_row < 192), 1.0, 0.0).astype(jnp.bfloat16)

    run = 16

    def recur(i, carry):
        older, newer = carry
        rows = pl.ds(pl.multiple_of(i * run * blocks, run * blocks), run * blocks)
        kap = jnp.dot(pieces_ref[rows, :], spread, preferred_element_type=jnp.float32)
        for j in range(run):
            now = (kap[j * blocks : (j + 1) * blocks] * z_ref[...]) * newer - older
            for half in range(blocks // 8):
                at = pl.ds(half * 8 * (LBLK + GAP) + i * run + j, 8, stride=LBLK + GAP)
                for g in range(halves):
                    leg_ref[g, at, :] = now[half * 8 : half * 8 + 8, g * 128 : g * 128 + 128]
            older, newer = newer, now
        return older, newer

    lax.fori_loop(0, LBLK // run, recur, (starts_ref[0], starts_ref[1]))

    rows_all = parts * q_group
    row = lax.broadcasted_iota(jnp.int32, (rows_all, 128), 0)
    lane = lax.broadcasted_iota(jnp.int32, (rows_all, 128), 1)
    picked = (row % MGRP) * parts + row // q_group == lane
    row = lax.broadcasted_iota(jnp.int32, (rows_all, KDIM), 0)
    lane = lax.broadcasted_iota(jnp.int32, (rows_all, KDIM), 1)
    same_q = row % q_group == lane // cycles
    cyc = lax.broadcasted_iota(jnp.int32, (cycles, KDIM), 0)
    lane_c = lax.broadcasted_iota(jnp.int32, (cycles, KDIM), 1) % cycles
    tile = jnp.where(cyc == lane_c, 1.0, 0.0).astype(jnp.bfloat16)
    row_k = lax.broadcasted_iota(jnp.int32, (rows_all, 128), 0) % q_group // MGRP
    per_group = q_group // MGRP
    weights = []
    for g in range(groups):
        narrow = jnp.zeros((rows_all, cycles), jnp.float32)
        for k in range(per_group):
            pick = jnp.where(picked & (row_k == k), 1.0, 0.0).astype(jnp.bfloat16)
            narrow = narrow + lax.dot_general(
                pick, modes_ref[g * per_group + k], (((1,), (1,)), ((), ())),
                preferred_element_type=jnp.float32,
            )
        wide = jnp.dot(narrow.astype(jnp.bfloat16), tile, preferred_element_type=jnp.float32)
        weights.append(jnp.where(same_q, wide, 0.0).astype(jnp.bfloat16))

    def project(u, _):
        cols = pl.ds(pl.multiple_of(u * 2 * LBLK, 2 * LBLK), 2 * LBLK)
        sources = [
            pl.ds(pl.multiple_of((2 * u + x) * (LBLK + GAP), 8), LBLK) for x in range(2)
        ]
        spectra_rows = []
        for g in range(groups):
            first = pl.multiple_of((step * groups + g) * q_group, 8)
            p_rows = jnp.concatenate(
                [turned_ref[2 * u + x, pl.ds(first, q_group), :] for x in range(2)], axis=1
            ) * scale
            leg = jnp.concatenate(
                [
                    jnp.concatenate(
                        [leg_ref[g * (KDIM // 128) + h, src, :] for h in range(KDIM // 128)],
                        axis=1,
                    )
                    for src in sources
                ],
                axis=0,
            ).astype(jnp.bfloat16)
            out = lax.dot_general(
                weights[g], leg, (((1,), (1,)), ((), ())), preferred_element_type=jnp.float32
            )
            crossed = out.reshape(parts, q_group, 2 * LBLK) * p_rows[None]
            crossed = crossed.astype(jnp.bfloat16)
            harm_ref[:, g * q_group : (g + 1) * q_group, cols] = crossed
            spectra_rows.append(crossed.astype(jnp.float32))
        pair = 0
        for i in range(maps):
            for k in range(i, maps):
                total = acc_ref[pair, :, cols]
                for x in spectra_rows:
                    total = total + x[i] * x[k] + x[maps + i] * x[maps + k]
                acc_ref[pair, :, cols] = total
                pair += 1
        return 0

    lax.fori_loop(0, blocks // 2, project, 0)

    @pl.when(step == pl.num_programs(0) - 1)
    def _():
        share = cross_ref.shape[2]

        def finish(d, _):
            for part in range(share // LBLK):
                cols = pl.ds(pl.multiple_of(d * share + part * LBLK, LBLK), LBLK)
                cross_ref[d, : acc_ref.shape[0], part * LBLK : (part + 1) * LBLK] = jnp.sum(
                    acc_ref[:, :, cols], axis=1
                ).astype(cross_ref.dtype)
            return 0

        lax.fori_loop(0, cross_ref.shape[0], finish, 0)


def project_blocks(
    legendre_starts, m_float, first_l, prepared, maps_count, cycle_scale, blk_total
):
    modes, pieces, turned, z_row = prepared
    local_cols, block_count, cycles = legendre_starts.shape[1:]
    local_len = block_count * LBLK
    q_group = KDIM // cycles
    parts = 2 * maps_count
    pairs = maps_count * (maps_count + 1) // 2
    base_l = first_l.astype(jnp.float32) + LBLK * jnp.arange(block_count, dtype=jnp.float32)
    degree = base_l[None, :] - 1.0
    m_col = m_float[:, None]
    coef = jnp.sqrt((4.0 * degree * degree - 1.0) / ((degree - m_col) * (degree + m_col)))
    starts = jnp.stack([legendre_starts[0] / coef[:, :, None], legendre_starts[1]])
    starts = jnp.transpose(starts, (0, 2, 1, 3)).reshape(2, block_count, local_cols * cycles)
    groups = STEP_LANES // KDIM
    step_cols = groups * q_group
    dims = (block_count, cycles, maps_count, q_group, cycle_scale)
    pair_rows = -(-pairs // 8) * 8
    share = local_len // blk_total
    whole = lambda shape: pl.BlockSpec(shape, lambda i: (0,) * len(shape))
    return pl.pallas_call(
        functools.partial(spectra_kernel, dims),
        grid=(local_cols // step_cols,),
        out_shape=(
            jax.ShapeDtypeStruct((parts, local_cols, local_len), jnp.bfloat16),
            jax.ShapeDtypeStruct((blk_total, pair_rows, share), jnp.bfloat16),
        ),
        in_specs=[
            pl.BlockSpec((2, block_count, STEP_LANES), lambda i: (0, 0, i)),
            whole((1, STEP_LANES)),
            whole(turned.shape),
            whole(pieces.shape),
            pl.BlockSpec((step_cols // MGRP, cycles, 128), lambda i: (i, 0, 0)),
        ],
        out_specs=(
            pl.BlockSpec((parts, step_cols, local_len), lambda i: (0, i, 0)),
            whole((blk_total, pair_rows, share)),
        ),
        scratch_shapes=[
            pltpu.VMEM((STEP_LANES // 128, block_count * (LBLK + GAP), 128), jnp.float32),
            pltpu.VMEM((pairs, 8, local_len), jnp.float32),
        ],
        compiler_params=pltpu.CompilerParams(vmem_limit_bytes=60 * 1024 * 1024),
    )(starts, z_row, turned, pieces, modes)


def modes_kernel(
    totals, number_ref, sky_ref, first_ref, wr_ref, wi_ref, phase_ref,
    out_ref, pieces_ref, scales_ref, z_ref, rows_ref, turned_ref, held_ref, p_ref,
    send_sem, recv_sem,
):
    blk_total, map_total, factor = totals
    maps = sky_ref.shape[0]
    count = blk_total * map_total
    me_blk, me_map = lax.axis_index("blk"), lax.axis_index("map")
    me = me_blk * map_total + me_map
    share = RES // blk_total
    barrier = pltpu.get_barrier_semaphore()
    for i in range(1, count):
        peer = lax.rem(me + i, count)
        pl.semaphore_signal(
            barrier, inc=1,
            device_id={"blk": peer // map_total, "map": lax.rem(peer, map_total)},
            device_id_type=pl.DeviceIdType.MESH,
        )
    rows_ref[...] = jnp.zeros_like(rows_ref)
    first = first_ref[...]
    parity = (number_ref[me] - NSIDE + 1) % 2
    odd = jnp.full((MGRP, RES), parity, jnp.int32) == 1
    cosines = jnp.where(odd, phase_ref[:MGRP], 1.0)
    sines = jnp.where(odd, phase_ref[MGRP:], 0.0)
    for n in range(maps):
        section = lax.dot_general(
            sky_ref[n], first, (((0,), (0,)), ((), ())), preferred_element_type=jnp.float32
        )
        section = section.astype(jnp.bfloat16).astype(jnp.float32)
        part_re, part_im = section[:, :RES], section[:, RES:]
        for c in range(MGRP):
            wave_re = wr_ref[c].astype(jnp.float32)
            wave_im = wi_ref[c].astype(jnp.float32)
            real = jnp.sum(wave_re * part_re - wave_im * part_im, axis=0, keepdims=True)
            imag = jnp.sum(wave_re * part_im + wave_im * part_re, axis=0, keepdims=True)
            cos, sin = cosines[c : c + 1], sines[c : c + 1]
            row = c * 2 * maps + n
            rows_ref[row : row + 1, :] = factor * (cos * real + sin * imag)
            rows_ref[row + maps : row + maps + 1, :] = factor * (cos * imag - sin * real)
    turned_ref[...] = rows_ref[...].T.astype(jnp.bfloat16)
    pl.semaphore_wait(barrier, count - 1)

    def copy_to(peer, source):
        target_blk = peer // map_total
        return pltpu.make_async_remote_copy(
            src_ref=turned_ref.at[pl.ds(pl.multiple_of(target_blk * share, share), share)],
            dst_ref=held_ref.at[source],
            send_sem=send_sem.at[peer],
            recv_sem=recv_sem.at[source],
            device_id={"blk": target_blk, "map": lax.rem(peer, map_total)},
            device_id_type=pl.DeviceIdType.MESH,
        )

    for i in range(1, count):
        copy_to(lax.rem(me + i, count), me).start()
    held_ref[me] = turned_ref[pl.ds(pl.multiple_of(me_blk * share, share), share), :]
    prepare(blk_total, number_ref, pieces_ref, scales_ref, z_ref, p_ref)
    for i in range(1, count):
        peer = lax.rem(me + i, count)
        copy_to(peer, peer).wait_recv()
    for i in range(1, count):
        copy_to(lax.rem(me + i, count), me).wait_send()
    gathered = held_ref[...].astype(jnp.float32)
    out_ref[...] = jnp.swapaxes(gathered, 0, 1).astype(jnp.bfloat16)


def prepare(blk_total, number_ref, pieces_ref, scales_ref, z_ref, p_ref):
    blocks = scales_ref.shape[0]
    local_cols = MGRP * RES // blk_total
    lane = lax.broadcasted_iota(jnp.int32, z_ref.shape, 1) % number_ref.shape[0]
    numbers = jnp.zeros(z_ref.shape, jnp.int32)
    for r in range(number_ref.shape[0]):
        numbers = jnp.where(lane == r, number_ref[r], numbers)
    z_ref[...] = cycle_height(numbers)
    lane = lax.broadcasted_iota(jnp.int32, (blocks, 256), 1)
    piece = lane // local_cols
    column = lax.axis_index("blk") * local_cols + lane % local_cols
    m_row = (MSTART + RES * (column % MGRP) + column // MGRP).astype(jnp.float32)
    block = lax.broadcasted_iota(jnp.int32, (blocks, 256), 0)
    base = LSTART + (lax.axis_index("map") * blocks + block) * LBLK

    def setup(j, carry):
        p_prev, q_prev = carry
        degree = (base + j).astype(jnp.float32)
        num = 4.0 * degree * degree - 1.0
        den = (degree - m_row) * (degree + m_row)
        root = lax.rsqrt(num * den)
        kappa = p_prev * p_prev
        high = kappa.astype(jnp.bfloat16).astype(jnp.float32)
        rest = kappa - high
        mid = rest.astype(jnp.bfloat16).astype(jnp.float32)
        low = rest - mid
        pieces = jnp.where(piece == 0, high, jnp.where(piece == 1, mid, low))
        pieces_ref[pl.ds(pl.multiple_of(j * blocks, blocks), blocks), :] = pieces.astype(
            jnp.bfloat16
        )
        p_now = num * root * q_prev
        q_now = den * root * p_prev
        for half in range(blocks // 8):
            p_ref[pl.ds(half * 8 * (LBLK + GAP) + j, 8, stride=LBLK + GAP), :] = p_now[
                half * 8 : half * 8 + 8, :128
            ]
        return p_now, q_now

    one = jnp.ones((blocks, 256), jnp.float32)
    lax.fori_loop(0, LBLK, setup, (one, one), unroll=4)

    def turn(t, _):
        turned = p_ref[pl.ds(pl.multiple_of(t * (LBLK + GAP), 8), LBLK), :].T
        scales_ref[t] = turned[:local_cols]
        return 0

    lax.fori_loop(0, blocks, turn, 0)


def exchange_modes(sky_maps, cycle_number, block_count, blk_total, map_total):
    _, maps, cycle_len = sky_maps.shape
    first_table, wave_re, wave_im = constant_tables(cycle_len)
    m_value = MSTART + np.arange(MGRP)[:, None] * RES + np.arange(RES)[None, :]
    angle = np.float32(math.pi / cycle_len) * (m_value % (2 * cycle_len)).astype(np.float32)
    phase = jnp.asarray(np.concatenate([np.cos(angle), np.sin(angle)], axis=0))
    count = blk_total * map_total
    return pl.pallas_call(
        functools.partial(modes_kernel, (blk_total, map_total, 1.0 / math.sqrt(cycle_len))),
        out_shape=(
            jax.ShapeDtypeStruct((RES // blk_total, count, 128), jnp.bfloat16),
            jax.ShapeDtypeStruct((block_count * LBLK, 256), jnp.bfloat16),
            jax.ShapeDtypeStruct((block_count, MGRP * RES // blk_total, LBLK), jnp.float32),
            jax.ShapeDtypeStruct((1, STEP_LANES), jnp.float32),
        ),
        in_specs=[pl.BlockSpec(memory_space=pltpu.SMEM)]
        + [pl.BlockSpec(memory_space=pltpu.VMEM)] * 5,
        out_specs=(pl.BlockSpec(memory_space=pltpu.VMEM),) * 4,
        scratch_shapes=[
            pltpu.VMEM((128, RES), jnp.float32),
            pltpu.VMEM((RES, 128), jnp.bfloat16),
            pltpu.VMEM((count, RES // blk_total, 128), jnp.bfloat16),
            pltpu.VMEM((block_count * (LBLK + GAP), 128), jnp.float32),
            pltpu.SemaphoreType.DMA((count,)),
            pltpu.SemaphoreType.DMA((count,)),
        ],
        compiler_params=pltpu.CompilerParams(collective_id=0, has_side_effects=True),
    )(cycle_number, sky_maps.reshape(maps, RES, cycle_len // RES), first_table, wave_re, wave_im, phase)


def constant_tables(cycle_len):
    low_len = cycle_len // RES
    residue = np.arange(RES)
    angle = np.float32(2.0 * math.pi / RES) * (
        residue[:, None] * residue[None, :] % RES
    ).astype(np.float32)
    first = np.concatenate([np.cos(angle), -np.sin(angle)], axis=1)
    m_value = MSTART + RES * np.arange(MGRP)[:, None, None] + residue[None, None, :]
    turn = m_value * np.arange(low_len)[None, :, None] % cycle_len
    angle = np.float32(2.0 * math.pi / cycle_len) * turn.astype(np.float32)
    short = lambda table: jnp.asarray(table.astype(jnp.bfloat16))
    return short(first), short(np.cos(angle)), short(-np.sin(angle))


def total_kernel(blk_total, maps, part_ref, out_ref, held_ref, send_sem, recv_sem):
    me = lax.axis_index("blk")
    barrier = pltpu.get_barrier_semaphore()
    for i in range(1, blk_total):
        pl.semaphore_signal(
            barrier, inc=1, device_id={"blk": lax.rem(me + i, blk_total)},
            device_id_type=pl.DeviceIdType.MESH,
        )
    pl.semaphore_wait(barrier, blk_total - 1)

    def copy_to(peer, source):
        return pltpu.make_async_remote_copy(
            src_ref=part_ref.at[peer],
            dst_ref=held_ref.at[source],
            send_sem=send_sem.at[peer],
            recv_sem=recv_sem.at[source],
            device_id={"blk": peer},
            device_id_type=pl.DeviceIdType.MESH,
        )

    order = [lax.rem(me + i, blk_total) for i in range(1, blk_total)]
    for peer in order:
        copy_to(peer, me).start()
    total = part_ref[me].astype(jnp.float32)
    for peer in order:
        copy_to(peer, peer).wait_recv()
        total = total + held_ref[peer].astype(jnp.float32)
    total = total * (1.0 / (MGRP * RES))
    pair = 0
    for i in range(maps):
        for k in range(i, maps):
            out_ref[i, k] = total[pair : pair + 1]
            if k > i:
                out_ref[k, i] = total[pair : pair + 1]
            pair += 1
    for peer in order:
        copy_to(peer, me).wait_send()


def total_cross(cross, maps):
    blk_total, pair_rows, share = cross.shape
    return pl.pallas_call(
        functools.partial(total_kernel, blk_total, maps),
        out_shape=jax.ShapeDtypeStruct((maps, maps, 1, share), jnp.float32),
        in_specs=[pl.BlockSpec(memory_space=pltpu.VMEM)],
        out_specs=pl.BlockSpec(memory_space=pltpu.VMEM),
        scratch_shapes=[
            pltpu.VMEM(cross.shape, cross.dtype),
            pltpu.SemaphoreType.DMA((blk_total,)),
            pltpu.SemaphoreType.DMA((blk_total,)),
        ],
        compiler_params=pltpu.CompilerParams(collective_id=1, has_side_effects=True),
    )(cross)


def kernel_fits(own_cycles, blk_total, cycles, maps_count, block_count):
    local_cols = MGRP * RES // blk_total
    return (
        own_cycles == 1
        and local_cols == 64
        and KDIM % cycles == 0
        and KDIM // cycles == 8
        and 2 * maps_count * MGRP <= 128
        and block_count % 8 == 0
        and block_count % blk_total == 0
    )


def fast_body(sky_maps, cycle_number, legendre_starts):
    _, maps_count, _ = sky_maps.shape
    map_total = lax.axis_size("map")
    blk_total = lax.axis_size("blk")
    local_cols, block_count, cycles = legendre_starts.shape[1:]
    prepared = exchange_modes(sky_maps, cycle_number, block_count, blk_total, map_total)
    column = lax.axis_index("blk") * local_cols + jnp.arange(local_cols, dtype=jnp.int32)
    m_float = (MSTART + RES * (column % MGRP) + column // MGRP).astype(jnp.float32)
    first_l = LSTART + lax.axis_index("map") * block_count * LBLK
    cycle_scale = 1.0 / math.sqrt(cycles)
    harmonics, cross = project_blocks(
        legendre_starts, m_float, first_l, prepared, maps_count, cycle_scale, blk_total
    )
    spectra = total_cross(cross, maps_count)
    return (jnp.transpose(harmonics, (1, 0, 2)), jnp.transpose(spectra, (2, 0, 1, 3)))


def body(sky_maps, cycle_number, legendre_starts):
    own_cycles, maps_count, cycle_len = sky_maps.shape
    map_total = lax.axis_size("map")
    blk_total = lax.axis_size("blk")
    cycles, block_count = cycle_number.shape[0], legendre_starts.shape[2]
    if kernel_fits(own_cycles, blk_total, cycles, maps_count, block_count):
        return fast_body(sky_maps, cycle_number, legendre_starts)
    tables = dft_tables(cycle_len)
    first_row = (lax.axis_index("blk") * map_total + lax.axis_index("map")) * own_cycles
    own_numbers = lax.dynamic_slice_in_dim(cycle_number, first_row, own_cycles)
    parity = (own_numbers - NSIDE + 1) % 2
    local_modes = cycle_transform(sky_maps, parity, tables)
    grouped = lax.all_gather(local_modes, "map", axis=0, tiled=True)
    regrouped = lax.all_to_all(grouped, "blk", split_axis=4, concat_axis=0, tiled=True)
    ordered = jnp.transpose(regrouped, (4, 3, 1, 2, 0))
    local_cols = ordered.shape[0] * ordered.shape[1]
    cycle_modes = ordered.reshape(local_cols, 2 * maps_count, -1)
    heights = cycle_height(cycle_number)
    column = lax.axis_index("blk") * local_cols + jnp.arange(local_cols, dtype=jnp.int32)
    m_float = (MSTART + RES * (column % MGRP) + column // MGRP).astype(jnp.float32)
    block_count = legendre_starts.shape[2]
    local_len = block_count * LBLK
    first_l = LSTART + lax.axis_index("map") * local_len
    cycle_scale = 1.0 / math.sqrt(cycle_modes.shape[-1])

    def one_block(block_index):
        start_pair = lax.dynamic_index_in_dim(legendre_starts, block_index, 2, keepdims=False)
        legendre_tile = legendre_rows(
            start_pair, heights, m_float, first_l + block_index * LBLK
        ).astype(jnp.bfloat16)
        projected = (
            jnp.einsum(
                "qlr,qnr->qnl", legendre_tile, cycle_modes, preferred_element_type=jnp.float32
            )
            * cycle_scale
        )
        return projected.astype(jnp.bfloat16)

    blocks_out = lax.map(one_block, jnp.arange(block_count, dtype=jnp.int32))
    harmonics = jnp.transpose(blocks_out, (1, 2, 0, 3)).reshape(
        local_cols, 2 * maps_count, local_len
    )
    total_cols = MGRP * RES
    spread = harmonics.reshape(local_cols, 2 * maps_count, blk_total, local_len // blk_total)
    spread = jnp.transpose(spread, (2, 3, 1, 0))
    received = lax.all_to_all(
        shortened(spread), "blk", split_axis=0, concat_axis=3, tiled=True
    ).astype(spread.dtype)
    item_count = received.shape[1]
    split_piece = received.reshape(item_count, 2, maps_count, received.shape[3])
    cross_sum = jnp.einsum(
        "gciq,gcjq->ijg", split_piece, split_piece, preferred_element_type=jnp.float32
    )
    owned = (cross_sum / total_cols)[None]
    return (harmonics, owned)


def solution(mesh):
    return jax.shard_map(
        body,
        mesh=mesh,
        in_specs=(P(("blk", "map"), None, None), P(), P(None, "blk", "map", None)),
        out_specs=(P("blk", None, "map"), P("map", None, None, "blk")),
        check_vma=False,
    )
```
